128 devices in a mesh: gx: 16 (over x, z), gy: 8 (over y, core).
Axes of the slice: x: 4, y: 4, z: 4, core: 2. Of those that a mesh axis runs over, the one named last changes fastest.
Arguments:
- old_states: float32 [32768, 12, 512], P(('gx', 'gy')), may hold values from -6 to 6
- new_place: int32 [32768], P(('gx', 'gy')), may hold values from -1 to 16383, as said below
- vectors_x: float32 [10, 10], replicated, may hold values from -2 to 2
- vectors_s: float32 [10, 10], replicated, may hold values from -2 to 2
- vectors_w: float32 [16, 10, 10], replicated, may hold values from -2 to 2
- values_x: float32 [10], replicated, may hold values from 0.2 to 5
- values_s: float32 [10], replicated, may hold values from 0.2 to 5
- values_w: float32 [16, 10], replicated, may hold values from 0.2 to 5
Outputs:
- new_states: float32 [64, 16, 16, 12, 512], P('gx', 'gy')
- correction: float32 [512, 128, 128], P('gx', 'gy')
The draws below stay inside these ranges and needn't reach their ends.
Inputs may be any that keep to these rules, and one draw needn't show every extreme that they name: `new_place`: every element number appears in exactly one slot; the other slots hold -1. One device's slots send at most 2 elements to any one device, and some pairs reach 2; some devices have all 256 slots filled.
All inputs are finite; a program needn't handle non-finite values.
Results may differ from the reference program's by a relative error of at most 0.00007.
Values sent between devices are 32-bit elements; how exact they have to be, the bound alone decides.
A program may use at most 128 MiB of HBM per device.

```python
import math
import jax
import jax.numpy as jnp
from jax import lax

NP = 8
EXT = 10
FIELDS = 12
BX = 4
BS = 2
EW = 16
E_DEV = 128
SLOTS = 256
NEX = 64
NES = 16
N_GX = 16
N_GY = 8


def shuffled(key_one, length):
    return jax.random.permutation(key_one, length)


def draw_new_place(key, part):
    devices = N_GX * N_GY
    heavy_n = devices // 4
    light_n = devices - heavy_n
    heavy_cap = 2 * E_DEV // devices
    light_cap = E_DEV // devices
    half_items = E_DEV // 2
    key_order = jax.random.fold_in(key, 11)
    key_local = jax.random.fold_in(key, 23)
    key_slots = jax.random.fold_in(key, 37)
    order = jax.random.permutation(key_order, devices).astype(jnp.int32)
    heavy_set = order[:heavy_n]
    light_set = order[heavy_n:]
    dest = jnp.arange(devices, dtype=jnp.int32)[:, None]
    item = jnp.arange(E_DEV, dtype=jnp.int32)[None, :]
    heavy_src = heavy_set[jnp.minimum(item, half_items - 1) // heavy_cap]
    light_pick = (dest + jnp.maximum(item - half_items, 0) // light_cap) % light_n
    light_src = light_set[light_pick]
    source = jnp.where(item < half_items, jnp.broadcast_to(heavy_src, (devices, E_DEV)), light_src)
    local_perm = jax.vmap(lambda one: shuffled(one, E_DEV))(jax.random.split(key_local, devices)).astype(jnp.int32)
    local_x = local_perm // (BS * EW)
    local_s = local_perm // EW % BS
    local_w = local_perm % EW
    dest_x = dest // N_GY
    dest_y = dest % N_GY
    global_id = ((dest_x * BX + local_x) * (BS * N_GY) + dest_y * BS + local_s) * EW + local_w
    source_flat = source.reshape(-1).astype(jnp.int32)
    global_flat = global_id.reshape(-1).astype(jnp.int32)
    item_total = devices * E_DEV
    sort_order = jnp.argsort(source_flat, stable=True)
    sorted_src = source_flat[sort_order]
    counts = jax.ops.segment_sum(jnp.ones((item_total,), jnp.int32), source_flat, devices)
    starts = jnp.cumsum(counts) - counts
    rank_sorted = jnp.arange(item_total, dtype=jnp.int32) - starts[sorted_src]
    bucket_rank = jnp.zeros((item_total,), jnp.int32).at[sort_order].set(rank_sorted)
    slot_perm = jax.vmap(lambda one: shuffled(one, SLOTS))(jax.random.split(key_slots, devices)).astype(jnp.int32)
    slot_of = slot_perm[source_flat, bucket_rank]
    placed = jnp.full((devices * SLOTS,), -1, jnp.int32).at[source_flat * SLOTS + slot_of].set(global_flat)
    return placed.astype(jnp.int32)


def steps_of(rng, shape, cuts, least, high):
    loudness = 1.0
    for position, shards_of in cuts:
        steps = jax.random.uniform(jax.random.fold_in(jax.random.fold_in(rng, 6), position), (shards_of,), jnp.float32, least / len(cuts), high / len(cuts))
        loudness = loudness * jnp.repeat(jnp.exp(steps), shape[position] // shards_of).reshape((-1,) + (1,) * (len(shape) - 1 - position))
    return loudness


def gaussian(key, shape, deviation, limit, shards=(), held_as=jnp.bfloat16):
    level = steps_of(key, shape, shards, -0.22, 0.18) if shards else 1.0
    values = jax.random.normal(key, shape, jnp.float32) * deviation * level
    return jnp.minimum(jnp.maximum(values, -limit), limit).astype(held_as)


def setup_inputs(seed: int = 0) -> dict:
    key_list = jax.random.split(jax.random.key(seed), 9)
    old_states = gaussian(key_list[0], (SLOTS * N_GX * N_GY, FIELDS, NP**3), 1.0, 6.0, ((0, 128),), jnp.float32)
    new_place = draw_new_place(jax.random.fold_in(key_list[8], 71), 0)
    vectors_x = gaussian(key_list[2], (EXT, EXT), EXT ** -0.5, 2.0, (), jnp.float32)
    vectors_s = gaussian(key_list[3], (EXT, EXT), EXT ** -0.5, 2.0, (), jnp.float32)
    vectors_w = gaussian(key_list[4], (EW, EXT, EXT), EXT ** -0.5, 2.0, (), jnp.float32)
    values_x = jnp.clip(jnp.exp(jax.random.uniform(key_list[5], (EXT,), jnp.float32, math.log(0.2), math.log(5.0))), 0.2, 5.0)
    values_s = jnp.clip(jnp.exp(jax.random.uniform(key_list[6], (EXT,), jnp.float32, math.log(0.2), math.log(5.0))), 0.2, 5.0)
    values_w = jnp.clip(jnp.exp(jax.random.uniform(key_list[7], (EW, EXT), jnp.float32, math.log(0.2), math.log(5.0))), 0.2, 5.0)
    return {"old_states": old_states, "new_place": new_place, "vectors_x": vectors_x, "vectors_s": vectors_s, "vectors_w": vectors_w, "values_x": values_x, "values_s": values_s, "values_w": values_w}


def windows(field, num_blocks, per_side):
    left_face = field[0:num_blocks * per_side:per_side]
    right_face = field[per_side + 1::per_side]
    core_cells = field[1:num_blocks * per_side + 1].reshape((num_blocks, per_side) + field.shape[1:])
    return jnp.concatenate([left_face[:, None], core_cells, right_face[:, None]], axis=1)


def unwindows(windowed, num_blocks, per_side):
    trailing = windowed.shape[2:]
    core_cells = windowed[:, 1:per_side + 1].reshape((num_blocks * per_side,) + trailing)
    result = jnp.zeros((num_blocks * per_side + 2,) + trailing, jnp.float32)
    result = result.at[1:num_blocks * per_side + 1].set(core_cells)
    result = result.at[0:num_blocks * per_side:per_side].add(windowed[:, 0])
    result = result.at[per_side + 1::per_side].add(windowed[:, per_side + 1])
    return result


def extend(padded, blocks, per_side):
    result = padded
    for which in range(3):
        turned = jnp.moveaxis(result, 2 * which, 0)
        turned = windows(turned, blocks[which], per_side)
        result = jnp.moveaxis(turned, (0, 1), (2 * which, 2 * which + 1))
    extent = per_side + 2
    result = jnp.transpose(result, (1, 3, 5, 0, 2, 4))
    return result.reshape(extent, extent, extent, blocks[0] * blocks[1] * blocks[2])


def retract(boxes, blocks, per_side):
    extent = per_side + 2
    result = boxes.reshape(extent, extent, extent, blocks[0], blocks[1], blocks[2])
    result = jnp.transpose(result, (3, 0, 4, 1, 5, 2))
    for which in (2, 1, 0):
        turned = jnp.moveaxis(result, (2 * which, 2 * which + 1), (0, 1))
        turned = unwindows(turned, blocks[which], per_side)
        result = jnp.moveaxis(turned, 0, 2 * which)
    return result


def rim_mask(extent):
    offset = jnp.arange(extent)
    on_rim = ((offset == 0) | (offset == extent - 1)).astype(jnp.int32)
    rim_count = on_rim[:, None, None] + on_rim[None, :, None] + on_rim[None, None, :]
    return (rim_count <= 1).astype(jnp.float32)[..., None]


def diag_solve(extended, vectors_x, vectors_s, stacked_w, values_x, values_s, stacked_values):
    highest = lax.Precision.HIGHEST
    section = jnp.einsum('ui,uvwn->ivwn', vectors_x, extended, precision=highest)
    section = jnp.einsum('vj,ivwn->ijwn', vectors_s, section, precision=highest)
    section = jnp.einsum('wkn,ijwn->ijkn', stacked_w, section, precision=highest)
    denom = values_x[:, None, None, None] + values_s[None, :, None, None] + stacked_values[None, None, :, :]
    modal = section / denom
    section = jnp.einsum('ui,ijkn->ujkn', vectors_x, modal, precision=highest)
    section = jnp.einsum('vj,ujkn->uvkn', vectors_s, section, precision=highest)
    return jnp.einsum('wkn,uvkn->uvwn', stacked_w, section, precision=highest)


def reference(old_states, new_place, vectors_x, vectors_s, vectors_w, values_x, values_s, values_w):
    element_total = NEX * NES * EW
    target_row = jnp.where(new_place < 0, element_total, new_place).astype(jnp.int32)
    new_flat = jnp.zeros((element_total, FIELDS, NP ** 3), jnp.float32).at[target_row].set(old_states, mode='drop')
    new_states = new_flat.reshape(NEX, NES, EW, FIELDS, NP ** 3)
    pressure = 3.0 * new_flat[:, 0] - 3.0 * new_flat[:, 1] + new_flat[:, 2]
    cell_field = pressure.reshape(NEX, NES, EW, NP, NP, NP).transpose(0, 3, 1, 4, 2, 5).reshape(NEX * NP, NES * NP, EW * NP)
    padded = jnp.pad(cell_field, ((1, 1), (1, 1), (0, 0)), mode='wrap')
    padded = jnp.pad(padded, ((0, 0), (0, 0), (1, 1)))
    blocks = (NEX, NES, EW)
    box_mask = rim_mask(NP + 2)
    extended = extend(padded, blocks, NP) * box_mask
    repeat = NEX * NES
    stacked_w = jnp.transpose(jnp.tile(vectors_w, (repeat, 1, 1)), (1, 2, 0))
    stacked_values = jnp.tile(values_w, (repeat, 1)).T
    local_fix = diag_solve(extended, vectors_x, vectors_s, stacked_w, values_x, values_s, stacked_values) * box_mask
    returned = retract(local_fix, blocks, NP)
    returned = returned.at[1].add(returned[-1]).at[-2].add(returned[0])
    returned = returned.at[:, 1].add(returned[:, -1]).at[:, -2].add(returned[:, 0])
    correction = returned[1:-1, 1:-1, 1:-1]
    return new_states, correction
```

```python
import functools
import jax
import jax.numpy as jnp
from jax import lax
from jax.experimental import pallas as pl
from jax.experimental.pallas import tpu as pltpu
from jax.sharding import PartitionSpec as P

MESH = pl.DeviceIdType.MESH
HIGHEST = lax.Precision.HIGHEST
F32 = jnp.float32

FIELDS = 12
FPC = 4
NCH = FIELDS // FPC
W = 4 * FPC
ROWS = 256
MB = 1024 * 1024


def send_order():
    left = [
        (a, b, c) for a in range(4) for b in range(4) for c in range(4) if (a, b, c) != (0, 0, 0)
    ]
    load = [0] * 6
    order = []

    def with_step(step):
        out = list(load)
        for axis, value in enumerate(step):
            if value in (1, 2):
                out[2 * axis] += 1
            if value in (2, 3):
                out[2 * axis + 1] += 1
        return out

    def cost(step):
        after = with_step(step)
        total = sum(after)
        return (6 * max(after) - total, sum(v * v for v in after) * 6 - total * total, step)

    while left:
        best = min(left, key=cost)
        left.remove(best)
        load[:] = with_step(best)
        order.append(best)
    return order


ORDER = send_order()


def my_place():
    gx = lax.axis_index("gx")
    gy = lax.axis_index("gy")
    return gx, gy


def peers():
    gx, gy = my_place()
    x, z = gx // 4, lax.rem(gx, 4)
    y, core = gy // 2, lax.rem(gy, 2)
    other = 1 - core
    out = [(gx, y * 2 + other)]
    for to_core in (core, other):
        for step in ORDER:
            hop = [step[i] * (1 - core) + (4 - step[i]) * core for i in range(3)]
            px = lax.rem(x + hop[0], 4)
            py = lax.rem(y + hop[1], 4)
            pz = lax.rem(z + hop[2], 4)
            out.append((px * 4 + pz, py * 2 + to_core))
    return out


def pack_kernel(place_ref, old_ref, out_ref, marks_ref, idx_v, idx_s, sem):
    @pl.when(pl.program_id(0) == 0)
    def _():
        place = place_ref[...]
        live = place >= 0
        p = jnp.maximum(place, 0)
        layer = p & 15
        es = (p >> 4) & 15
        ex = p >> 8
        target = ((ex >> 2) * 8 + (es >> 1)).astype(F32)
        row = (((ex & 3) * 2 + (es & 1)) * 16 + layer).astype(F32)
        key = jnp.where(live, target, -1.0)
        ri = lax.broadcasted_iota(jnp.int32, (ROWS, ROWS), 0)
        ci = lax.broadcasted_iota(jnp.int32, (ROWS, ROWS), 1)
        rf = ri.astype(F32)
        cf = ci.astype(F32)
        same = ri == ci
        key_b = jnp.broadcast_to(key, (ROWS, ROWS))
        key_c = jnp.sum(jnp.where(same, key_b, 0.0), axis=1, keepdims=True)
        rank = jnp.sum(
            jnp.where((key_c == key_b) & (ri < ci), 1.0, 0.0), axis=0, keepdims=True
        )
        pos = jnp.where(live, target * 2.0 + rank, -1.0)
        pos_b = jnp.broadcast_to(pos, (ROWS, ROWS))
        pos_c = jnp.sum(jnp.where(same, pos_b, 0.0), axis=1, keepdims=True)
        idx = jnp.sum(jnp.where(pos_c == cf, rf, 0.0), axis=0, keepdims=True)
        idx_v[...] = idx.astype(jnp.int32)
        row_b = jnp.broadcast_to(row + 1.0, (ROWS, ROWS))
        mark = jnp.sum(jnp.where(pos_b == rf, row_b, 0.0), axis=1, keepdims=True) - 1.0
        marks_ref[...] = jnp.broadcast_to(mark, (ROWS, 128))
        copy = pltpu.make_async_copy(idx_v, idx_s, sem)
        copy.start()
        copy.wait()

    def body(step, _):
        for more in range(4):
            r = step * 4 + more
            s = idx_s[0, r]
            base = (s >> 3) * 32 + (s & 7)
            for f in range(FPC):
                out_ref[0, r, 4 * f : 4 * f + 4, :] = old_ref[f, pl.ds(base, 4, stride=8), :]
        return 0

    lax.fori_loop(0, ROWS // 4, body, 0)


def pack(new_place, old_view):
    return pl.pallas_call(
        pack_kernel,
        grid=(NCH,),
        in_specs=[
            pl.BlockSpec((1, ROWS), lambda c: (0, 0)),
            pl.BlockSpec((FPC, ROWS * 4, 128), lambda c: (c, 0, 0)),
        ],
        out_specs=[
            pl.BlockSpec((1, ROWS, W, 128), lambda c: (c, 0, 0, 0)),
            pl.BlockSpec((ROWS, 128), lambda c: (0, 0)),
        ],
        out_shape=[
            jax.ShapeDtypeStruct((NCH, ROWS, W, 128), F32),
            jax.ShapeDtypeStruct((ROWS, 128), F32),
        ],
        scratch_shapes=[
            pltpu.VMEM((1, ROWS), jnp.int32),
            pltpu.SMEM((1, ROWS), jnp.int32),
            pltpu.SemaphoreType.DMA,
        ],
        name="pack",
    )(new_place, old_view)


def migrate_kernel(src, marks, dst, marks_out, ssem, rsem, msem_s, msem_r, lsem):
    gx, gy = my_place()
    me = gx * 8 + gy
    everyone = peers()
    barrier = pltpu.get_barrier_semaphore()

    def greet(k, _):
        d = lax.rem(me + k, 128)
        pl.semaphore_signal(
            barrier, inc=1, device_id=(d // 8, lax.rem(d, 8)), device_id_type=MESH
        )
        return 0

    lax.fori_loop(1, 128, greet, 0)
    own = []
    for ch in range(NCH):
        own.append(
            pltpu.make_async_copy(
                src.at[ch, pl.ds(2 * me, 2)], dst.at[ch, pl.ds(2 * me, 2)], lsem.at[ch]
            )
        )
    own.append(
        pltpu.make_async_copy(
            marks.at[pl.ds(2 * me, 2)], marks_out.at[pl.ds(2 * me, 2)], lsem.at[NCH]
        )
    )
    for copy in own:
        copy.start()
    pl.semaphore_wait(barrier, 127)
    for peer in everyone:
        d = peer[0] * 8 + peer[1]
        pltpu.make_async_remote_copy(
            marks.at[pl.ds(2 * d, 2)],
            marks_out.at[pl.ds(2 * me, 2)],
            msem_s,
            msem_r,
            device_id=peer,
            device_id_type=MESH,
        ).start()

    def chunk(ch, _):
        for peer in everyone:
            d = peer[0] * 8 + peer[1]
            pltpu.make_async_remote_copy(
                src.at[ch, pl.ds(2 * d, 2)],
                dst.at[ch, pl.ds(2 * me, 2)],
                ssem.at[ch],
                rsem.at[ch],
                device_id=peer,
                device_id_type=MESH,
            ).start()
        return 0

    lax.fori_loop(0, NCH, chunk, 0)
    some = pl.ds(0, ROWS - 2)
    pltpu.make_async_copy(marks.at[some], marks_out.at[some], msem_r).wait()
    pltpu.make_async_copy(marks.at[some], marks_out.at[some], msem_s).wait()
    for ch in range(NCH):
        pltpu.make_async_copy(src.at[ch, some], dst.at[ch, some], rsem.at[ch]).wait()
        pltpu.make_async_copy(src.at[ch, some], dst.at[ch, some], ssem.at[ch]).wait()
    for copy in own:
        copy.wait()


def migrate(packed, marks):
    marks = marks.reshape(ROWS, 1, 128)
    return pl.pallas_call(
        migrate_kernel,
        in_specs=[pl.BlockSpec(memory_space=pl.ANY)] * 2,
        out_specs=[pl.BlockSpec(memory_space=pl.ANY)] * 2,
        out_shape=[
            jax.ShapeDtypeStruct(packed.shape, F32),
            jax.ShapeDtypeStruct(marks.shape, F32),
        ],
        scratch_shapes=[
            pltpu.SemaphoreType.DMA((NCH,)),
            pltpu.SemaphoreType.DMA((NCH,)),
            pltpu.SemaphoreType.DMA,
            pltpu.SemaphoreType.DMA,
            pltpu.SemaphoreType.DMA((NCH + 1,)),
        ],
        compiler_params=pltpu.CompilerParams(collective_id=1, has_side_effects=True),
        name="migrate",
    )(packed, marks)


def unpack_kernel(marks_ref, recv_ref, out_ref, idx_v, idx_s, sem):
    @pl.when(pl.program_id(0) == 0)
    def _():
        rf = lax.broadcasted_iota(jnp.int32, (ROWS, 128), 0).astype(F32)
        nf = lax.broadcasted_iota(jnp.int32, (ROWS, 128), 1).astype(F32)
        idx = jnp.sum(jnp.where(marks_ref[...] == nf, rf, 0.0), axis=0, keepdims=True)
        idx_v[...] = idx.astype(jnp.int32)
        copy = pltpu.make_async_copy(idx_v, idx_s, sem)
        copy.start()
        copy.wait()

    def body(col, _):
        for layer in range(16):
            a = idx_s[0, col * 16 + layer]
            for f in range(FPC):
                start = (layer // 8) * 32 + layer % 8
                out_ref[col, f, pl.ds(start, 4, stride=8), :] = recv_ref[
                    0, a, 4 * f : 4 * f + 4, :
                ]
        return 0

    lax.fori_loop(0, 8, body, 0)


def unpack(marks, recv):
    return pl.pallas_call(
        unpack_kernel,
        grid=(NCH,),
        in_specs=[
            pl.BlockSpec((ROWS, 128), lambda c: (0, 0)),
            pl.BlockSpec((1, ROWS, W, 128), lambda c: (c, 0, 0, 0)),
        ],
        out_specs=pl.BlockSpec((8, FPC, 64, 128), lambda c: (0, c, 0, 0)),
        out_shape=jax.ShapeDtypeStruct((8, FIELDS, 64, 128), F32),
        scratch_shapes=[
            pltpu.VMEM((1, 128), jnp.int32),
            pltpu.SMEM((1, 128), jnp.int32),
            pltpu.SemaphoreType.DMA,
        ],
        name="unpack",
    )(marks, recv)


def lane_iota(rows):
    return lax.broadcasted_iota(jnp.int32, (rows, 128), 1)


def tile_of(k):
    return slice(k * 128, (k + 1) * 128)


def build_tables(vx, vs, vw, valx, vals, valw, pad, mat, mat_t, coef, wval, dcol):
    q = lax.broadcasted_iota(jnp.int32, (16, 128), 1)
    u_row = lax.broadcasted_iota(jnp.int32, (16, 128), 0)
    along = (q & 7) + 1
    u_of = jnp.where(q < 64, (q >> 3) + 1, jnp.where(q < 72, 0, jnp.where(q < 80, 9, along)))
    v_of = jnp.where(q < 80, along, jnp.where(q < 88, 0, 9))
    pick_u = jnp.where((u_row == u_of) & (q < 96), 1.0, 0.0)
    pick_v = jnp.where((u_row == v_of) & (q < 96), 1.0, 0.0)
    big_r = lax.broadcasted_iota(jnp.int32, (128, 128), 0)
    big_c = lax.broadcasted_iota(jnp.int32, (128, 128), 1)
    i_of = (big_r * 205) >> 11
    j_of = big_r - i_of * 10
    pick_i = jnp.where((big_c == i_of) & (big_r < 100), 1.0, 0.0)
    pick_j = jnp.where((big_c == j_of) & (big_r < 100), 1.0, 0.0)
    first = (((0,), (0,)), ((), ()))

    def padded(value, width=10):
        pad[...] = jnp.zeros((16, 128), F32)
        pad[0 : value.shape[0], 0:width] = value
        return pad[...]

    def grow(vec, pick_q, pick_row):
        side = lax.dot_general(
            padded(vec), pick_q, first, precision=HIGHEST, preferred_element_type=F32
        )
        return jnp.dot(pick_row, side, precision=HIGHEST, preferred_element_type=F32)

    both = grow(vx[...], pick_u, pick_i) * grow(vs[...], pick_v, pick_j)
    mat[...] = both
    mat_t[...] = both.T
    rows = padded(valx[...])[0:1, :]
    d = jnp.sum(pick_i * rows, axis=1, keepdims=True)
    rows = padded(vals[...])[0:1, :]
    d = d + jnp.sum(pick_j * rows, axis=1, keepdims=True)
    dcol[...] = jnp.broadcast_to(d, (128, 128))
    spread = jnp.where(u_row == (q & 15), 1.0, 0.0)
    for w in range(10):
        table = lax.dot_general(
            padded(vw[w]), spread, first, precision=HIGHEST, preferred_element_type=F32
        )
        for k in range(10):
            coef[w, k] = jnp.broadcast_to(table[k : k + 1, :], (8, 128))
    table = lax.dot_general(
        padded(valw[...]), spread, first, precision=HIGHEST, preferred_element_type=F32
    )
    for k in range(10):
        wval[k] = jnp.broadcast_to(table[k : k + 1, :], (8, 128))


def right_side(arrived, marks, points):
    nf = lane_iota(ROWS).astype(F32)
    chosen = jnp.where(marks == nf, 1.0, 0.0)
    for c in range(4):
        f0, f1, f2 = (arrived[pl.ds(4 * f + c, ROWS, stride=W), :] for f in range(3))
        rows = 3.0 * f0 - 3.0 * f1 + f2
        points[128 * c : 128 * (c + 1), :] = jnp.dot(
            rows.T, chosen, precision=HIGHEST, preferred_element_type=F32
        )


def gather_planes(points, planes):
    for i in range(8):
        planes[0, 8 * i : 8 * i + 8, :] = points[64 * i + 56 : 64 * i + 64, :]
        planes[1, 8 * i : 8 * i + 8, :] = points[64 * i : 64 * i + 8, :]


def neighbours():
    gx, gy = my_place()
    return (
        (lax.rem(gx + 1, 16), gy),
        (lax.rem(gx + 15, 16), gy),
        (gx, lax.rem(gy + 1, 8)),
        (gx, lax.rem(gy + 7, 8)),
    )


def plane_copies(sources, target, ssem, rsem, base):
    return [
        pltpu.make_async_remote_copy(
            sources[p],
            target.at[p],
            ssem.at[base + p],
            rsem.at[base + p],
            device_id=peer,
            device_id_type=MESH,
        )
        for p, peer in enumerate(neighbours())
    ]


def fill_inner(points, boxes):
    boxes[96:128, :] = jnp.zeros((32, 1280), F32)
    boxes[64:96, tile_of(0)] = jnp.zeros((32, 128), F32)
    boxes[64:96, tile_of(9)] = jnp.zeros((32, 128), F32)
    layer = lane_iota(64) & 15
    for k in range(8):
        value = points[pl.ds(k, 64, stride=8), :]
        boxes[0:64, tile_of(k + 1)] = value
        if k == 7:
            boxes[0:64, tile_of(0)] = jnp.where(layer == 0, 0.0, pltpu.roll(value, 1, 1))
        if k == 0:
            boxes[0:64, tile_of(9)] = jnp.where(layer == 15, 0.0, pltpu.roll(value, 127, 1))


def fill_faces(points, planes, arrived, boxes):
    lane = lane_iota(8)
    upper = (lane & 16) != 0
    for k in range(8):
        own = points[pl.ds(448 + k, 8, stride=8), :]
        far = arrived[0, pl.ds(k, 8, stride=8), :]
        boxes[64:72, tile_of(k + 1)] = pltpu.roll(jnp.where(lane >= 96, far, own), 32, 1)
        own = points[pl.ds(k, 8, stride=8), :]
        far = arrived[1, pl.ds(k, 8, stride=8), :]
        boxes[72:80, tile_of(k + 1)] = pltpu.roll(jnp.where(lane < 32, far, own), 96, 1)
        own = planes[0, pl.ds(k, 8, stride=8), :]
        far = arrived[2, pl.ds(k, 8, stride=8), :]
        boxes[80:88, tile_of(k + 1)] = jnp.where(
            upper, pltpu.roll(own, 16, 1), pltpu.roll(far, 112, 1)
        )
        own = planes[1, pl.ds(k, 8, stride=8), :]
        far = arrived[3, pl.ds(k, 8, stride=8), :]
        boxes[88:96, tile_of(k + 1)] = jnp.where(
            upper, pltpu.roll(far, 16, 1), pltpu.roll(own, 112, 1)
        )


def solve_boxes(boxes, half, mat, mat_t, coef, wval, dcol):
    half[0:104, :] = jnp.dot(
        mat[0:104, :], boxes[...], precision=HIGHEST, preferred_element_type=F32
    )
    half[104:128, :] = jnp.zeros((24, 1280), F32)

    def rows(t, _):
        at = pl.ds(pl.multiple_of(t * 8, 8), 8)
        section = [half[at, tile_of(w)] for w in range(10)]
        modal = []
        for k in range(10):
            total = coef[0, k] * section[0]
            for w in range(1, 10):
                total = total + coef[w, k] * section[w]
            modal.append(total / (dcol[at, :] + wval[k]))
        for w in range(10):
            total = coef[w, 0] * modal[0]
            for k in range(1, 10):
                total = total + coef[w, k] * modal[k]
            half[at, tile_of(w)] = total
        return 0

    lax.fori_loop(0, 13, rows, 0)
    boxes[0:96, :] = jnp.dot(
        mat_t[0:96, :], half[...], precision=HIGHEST, preferred_element_type=F32
    )


def return_planes(boxes, planes):
    for p, first in enumerate((72, 64, 88, 80)):
        for k in range(8):
            planes[p, pl.ds(k, 8, stride=8), :] = boxes[first : first + 8, tile_of(k + 1)]


def sum_cells(planes, arrived, boxes, sums, out):
    lane = lane_iota(8)
    upper = (lane & 16) != 0
    layer = lane_iota(64) & 15
    for k in range(8):
        value = boxes[0:64, tile_of(k + 1)]
        if k == 7:
            value = value + jnp.where(
                layer == 15, 0.0, pltpu.roll(boxes[0:64, tile_of(0)], 127, 1)
            )
        if k == 0:
            value = value + jnp.where(layer == 0, 0.0, pltpu.roll(boxes[0:64, tile_of(9)], 1, 1))
        sums[k] = value
        at = pl.ds(k, 8, stride=8)
        own, far = planes[0, at, :], arrived[0, at, :]
        sums[k, 0:8, :] += pltpu.roll(jnp.where(lane >= 96, far, own), 32, 1)
        own, far = planes[1, at, :], arrived[1, at, :]
        sums[k, 56:64, :] += pltpu.roll(jnp.where(lane < 32, far, own), 96, 1)
        own, far = planes[2, at, :], arrived[2, at, :]
        sums[k, pl.ds(0, 8, stride=8), :] += jnp.where(
            upper, pltpu.roll(own, 16, 1), pltpu.roll(far, 112, 1)
        )
        own, far = planes[3, at, :], arrived[3, at, :]
        sums[k, pl.ds(7, 8, stride=8), :] += jnp.where(
            upper, pltpu.roll(far, 16, 1), pltpu.roll(own, 112, 1)
        )
    src = lax.broadcasted_iota(jnp.int32, (128, 128), 0)
    to = lax.broadcasted_iota(jnp.int32, (128, 128), 1)
    order = jnp.where(to == (src & 15) * 8 + (src >> 4), 1.0, 0.0)
    group = lane_iota(64) >> 4
    for b in range(8):
        mixed = jnp.zeros((64, 128), F32)
        for k in range(8):
            turned = pltpu.roll(sums[k], ((k - b) % 8) * 16, 1) if k != b else sums[k]
            mixed = jnp.where(group == k, turned, mixed)
        mixed = jnp.dot(mixed, order, precision=HIGHEST, preferred_element_type=F32)
        for i in range(8):
            first = ((b // 2) * 8 + i) * 16 + (b % 2) * 8
            out[first : first + 8, :] = mixed[8 * i : 8 * i + 8, :]


def sweep_kernel(
    arrived, marks, vx, vs, vw, valx, vals, valw, out,
    pad, mat, mat_t, coef, wval, dcol, points, faces, faces_in, boxes, half,
    planes, planes_in, sums, ssem, rsem,
):
    barrier = pltpu.get_barrier_semaphore()
    for peer in neighbours():
        pl.semaphore_signal(barrier, inc=1, device_id=peer, device_id_type=MESH)
    build_tables(vx, vs, vw, valx, vals, valw, pad, mat, mat_t, coef, wval, dcol)
    right_side(arrived.at[0], marks[...], points)
    gather_planes(points, faces)
    pl.semaphore_wait(barrier, 4)
    sources = (points.at[pl.ds(448, 64)], points.at[pl.ds(0, 64)], faces.at[0], faces.at[1])
    copies = plane_copies(sources, faces_in, ssem, rsem, 0)
    for copy in copies:
        copy.start()
    fill_inner(points, boxes)
    for copy in copies:
        copy.wait()
    fill_faces(points, faces, faces_in, boxes)
    solve_boxes(boxes, half, mat, mat_t, coef, wval, dcol)
    return_planes(boxes, planes)
    copies = plane_copies([planes.at[p] for p in range(4)], planes_in, ssem, rsem, 4)
    for copy in copies:
        copy.start()
    for copy in copies:
        copy.wait()
    sum_cells(planes, planes_in, boxes, sums, out)


SWEEP_SCRATCH = [
    pltpu.VMEM((16, 128), F32),
    pltpu.VMEM((128, 128), F32),
    pltpu.VMEM((128, 128), F32),
    pltpu.VMEM((10, 10, 8, 128), F32),
    pltpu.VMEM((10, 8, 128), F32),
    pltpu.VMEM((128, 128), F32),
    pltpu.VMEM((512, 128), F32),
    pltpu.VMEM((2, 64, 128), F32),
    pltpu.VMEM((4, 64, 128), F32),
    pltpu.VMEM((128, 1280), F32),
    pltpu.VMEM((128, 1280), F32),
    pltpu.VMEM((4, 64, 128), F32),
    pltpu.VMEM((4, 64, 128), F32),
    pltpu.VMEM((8, 64, 128), F32),
    pltpu.SemaphoreType.DMA((8,)),
    pltpu.SemaphoreType.DMA((8,)),
]


def sweep(recv, marks, tables):
    whole = pl.BlockSpec(memory_space=pltpu.VMEM)
    return pl.pallas_call(
        sweep_kernel,
        grid=(1,),
        in_specs=[pl.BlockSpec((1, ROWS * W, 128), lambda c: (0, 0, 0))] + [whole] * 7,
        out_specs=whole,
        out_shape=jax.ShapeDtypeStruct((512, 128), F32),
        scratch_shapes=SWEEP_SCRATCH,
        compiler_params=pltpu.CompilerParams(collective_id=2, has_side_effects=True),
        name="sweep",
    )(recv, marks, *tables)


def shards(old_states, new_place, vectors_x, vectors_s, vectors_w, values_x, values_s, values_w):
    old_view = old_states.transpose(1, 0, 2).reshape(FIELDS, 32, 8, 4, 128)
    old_view = old_view.transpose(0, 1, 3, 2, 4).reshape(FIELDS, ROWS * 4, 128)
    packed, marks = pack(new_place.reshape(1, ROWS), old_view)
    recv, marks_in = migrate(packed, marks)
    marks_in = marks_in.reshape(ROWS, 128)
    tables = (
        vectors_x,
        vectors_s,
        vectors_w.transpose(1, 0, 2),
        values_x.reshape(1, 10),
        values_s.reshape(1, 10),
        values_w,
    )
    correction = sweep(recv.reshape(NCH, ROWS * W, 128), marks_in, tables)
    placed = unpack(marks_in, recv)
    placed = placed.reshape(4, 2, FIELDS, 2, 4, 8, 128).transpose(0, 1, 3, 5, 2, 4, 6)
    return placed.reshape(4, 2, 16, FIELDS, 512), correction.reshape(32, 16, 128)


def solution(mesh):
    placed = (P(("gx", "gy"), None, None), P(("gx", "gy")), P(), P(), P(), P(), P(), P())
    return jax.shard_map(
        shards,
        mesh=mesh,
        in_specs=placed,
        out_specs=(P("gx", "gy", None, None, None), P("gx", "gy", None)),
        check_vma=False,
    )
```

```python
import functools
import jax
import jax.numpy as jnp
from jax import lax
from jax.experimental import pallas as pl
from jax.experimental.pallas import tpu as pltpu
from jax.sharding import PartitionSpec as P

MESH = pl.DeviceIdType.MESH
HIGHEST = lax.Precision.HIGHEST
F32 = jnp.float32

FIELDS = 12
FPC = 2
NCH = FIELDS // FPC
W = 4 * FPC
ROWS = 256


def send_order():
    left = [
        (a, b, c) for a in range(4) for b in range(4) for c in range(4) if (a, b, c) != (0, 0, 0)
    ]
    load = [0] * 6
    order = []

    def with_step(step):
        out = list(load)
        for axis, value in enumerate(step):
            if value in (1, 2):
                out[2 * axis] += 1
            if value in (2, 3):
                out[2 * axis + 1] += 1
        return out

    def cost(step):
        after = with_step(step)
        total = sum(after)
        return (6 * max(after) - total, sum(v * v for v in after) * 6 - total * total, step)

    while left:
        best = min(left, key=cost)
        left.remove(best)
        load[:] = with_step(best)
        order.append(best)
    return order


ORDER = send_order()


def my_place():
    gx = lax.axis_index("gx")
    gy = lax.axis_index("gy")
    return gx, gy


def peers():
    gx, gy = my_place()
    x, z = gx // 4, lax.rem(gx, 4)
    y, core = gy // 2, lax.rem(gy, 2)
    other = 1 - core
    out = [(gx, y * 2 + other)]
    for to_core in (core, other):
        for step in ORDER:
            hop = [step[i] * (1 - core) + (4 - step[i]) * core for i in range(3)]
            px = lax.rem(x + hop[0], 4)
            py = lax.rem(y + hop[1], 4)
            pz = lax.rem(z + hop[2], 4)
            out.append((px * 4 + pz, py * 2 + to_core))
    return out


def lane_iota(rows):
    return lax.broadcasted_iota(jnp.int32, (rows, 128), 1)


def tile_of(k):
    return slice(k * 128, (k + 1) * 128)


def build_tables(vx, vs, vw, valx, vals, valw, pad, mat, mat_t, coef, wval, dcol):
    q = lax.broadcasted_iota(jnp.int32, (16, 128), 1)
    u_row = lax.broadcasted_iota(jnp.int32, (16, 128), 0)
    along = (q & 7) + 1
    u_of = jnp.where(q < 64, (q >> 3) + 1, jnp.where(q < 72, 0, jnp.where(q < 80, 9, along)))
    v_of = jnp.where(q < 80, along, jnp.where(q < 88, 0, 9))
    pick_u = jnp.where((u_row == u_of) & (q < 96), 1.0, 0.0)
    pick_v = jnp.where((u_row == v_of) & (q < 96), 1.0, 0.0)
    big_r = lax.broadcasted_iota(jnp.int32, (128, 128), 0)
    big_c = lax.broadcasted_iota(jnp.int32, (128, 128), 1)
    i_of = (big_r * 205) >> 11
    j_of = big_r - i_of * 10
    pick_i = jnp.where((big_c == i_of) & (big_r < 100), 1.0, 0.0)
    pick_j = jnp.where((big_c == j_of) & (big_r < 100), 1.0, 0.0)
    first = (((0,), (0,)), ((), ()))

    def padded(value, width=10):
        pad[...] = jnp.zeros((16, 128), F32)
        pad[0 : value.shape[0], 0:width] = value
        return pad[...]

    def grow(vec, pick_q, pick_row):
        side = lax.dot_general(
            padded(vec), pick_q, first, precision=HIGHEST, preferred_element_type=F32
        )
        return jnp.dot(pick_row, side, precision=HIGHEST, preferred_element_type=F32)

    both = grow(vx[...], pick_u, pick_i) * grow(vs[...], pick_v, pick_j)
    mat[...] = both
    mat_t[...] = both.T
    rows = padded(valx[...])[0:1, :]
    d = jnp.sum(pick_i * rows, axis=1, keepdims=True)
    rows = padded(vals[...])[0:1, :]
    d = d + jnp.sum(pick_j * rows, axis=1, keepdims=True)
    dcol[...] = jnp.broadcast_to(d, (128, 128))
    spread = jnp.where(u_row == (q & 15), 1.0, 0.0)
    for w in range(10):
        table = lax.dot_general(
            padded(vw[w]), spread, first, precision=HIGHEST, preferred_element_type=F32
        )
        for k in range(10):
            coef[w, k] = jnp.broadcast_to(table[k : k + 1, :], (8, 128))
    table = lax.dot_general(
        padded(valw[...]), spread, first, precision=HIGHEST, preferred_element_type=F32
    )
    for k in range(10):
        wval[k] = jnp.broadcast_to(table[k : k + 1, :], (8, 128))


def right_side(arrived, marks, points):
    nf = lane_iota(ROWS).astype(F32)
    chosen = jnp.where(marks == nf, 1.0, 0.0)
    for c in range(4):
        f0, f1, f2 = (
            arrived[f // FPC][pl.ds(4 * (f % FPC) + c, ROWS, stride=W), :] for f in range(3)
        )
        rows = 3.0 * f0 - 3.0 * f1 + f2
        points[128 * c : 128 * (c + 1), :] = jnp.dot(
            rows.T, chosen, precision=HIGHEST, preferred_element_type=F32
        )


def gather_planes(points, planes):
    for i in range(8):
        planes[0, 8 * i : 8 * i + 8, :] = points[64 * i + 56 : 64 * i + 64, :]
        planes[1, 8 * i : 8 * i + 8, :] = points[64 * i : 64 * i + 8, :]


def neighbours():
    gx, gy = my_place()
    return (
        (lax.rem(gx + 1, 16), gy),
        (lax.rem(gx + 15, 16), gy),
        (gx, lax.rem(gy + 1, 8)),
        (gx, lax.rem(gy + 7, 8)),
    )


def plane_copies(sources, target, ssem, rsem, base):
    return [
        pltpu.make_async_remote_copy(
            sources[p],
            target.at[p],
            ssem.at[base + p],
            rsem.at[base + p],
            device_id=peer,
            device_id_type=MESH,
        )
        for p, peer in enumerate(neighbours())
    ]


def fill_inner(points, boxes):
    boxes[96:128, :] = jnp.zeros((32, 1280), F32)
    boxes[64:96, tile_of(0)] = jnp.zeros((32, 128), F32)
    boxes[64:96, tile_of(9)] = jnp.zeros((32, 128), F32)
    layer = lane_iota(64) & 15
    for k in range(8):
        value = points[pl.ds(k, 64, stride=8), :]
        boxes[0:64, tile_of(k + 1)] = value
        if k == 7:
            boxes[0:64, tile_of(0)] = jnp.where(layer == 0, 0.0, pltpu.roll(value, 1, 1))
        if k == 0:
            boxes[0:64, tile_of(9)] = jnp.where(layer == 15, 0.0, pltpu.roll(value, 127, 1))


def fill_faces(points, planes, arrived, boxes):
    lane = lane_iota(8)
    upper = (lane & 16) != 0
    for k in range(8):
        own = points[pl.ds(448 + k, 8, stride=8), :]
        far = arrived[0, pl.ds(k, 8, stride=8), :]
        boxes[64:72, tile_of(k + 1)] = pltpu.roll(jnp.where(lane >= 96, far, own), 32, 1)
        own = points[pl.ds(k, 8, stride=8), :]
        far = arrived[1, pl.ds(k, 8, stride=8), :]
        boxes[72:80, tile_of(k + 1)] = pltpu.roll(jnp.where(lane < 32, far, own), 96, 1)
        own = planes[0, pl.ds(k, 8, stride=8), :]
        far = arrived[2, pl.ds(k, 8, stride=8), :]
        boxes[80:88, tile_of(k + 1)] = jnp.where(
            upper, pltpu.roll(own, 16, 1), pltpu.roll(far, 112, 1)
        )
        own = planes[1, pl.ds(k, 8, stride=8), :]
        far = arrived[3, pl.ds(k, 8, stride=8), :]
        boxes[88:96, tile_of(k + 1)] = jnp.where(
            upper, pltpu.roll(far, 16, 1), pltpu.roll(own, 112, 1)
        )


def solve_boxes(boxes, half, mat, mat_t, coef, wval, dcol):
    half[0:104, :] = jnp.dot(
        mat[0:104, :], boxes[...], precision=HIGHEST, preferred_element_type=F32
    )
    half[104:128, :] = jnp.zeros((24, 1280), F32)

    def rows(t, _):
        at = pl.ds(pl.multiple_of(t * 8, 8), 8)
        section = [half[at, tile_of(w)] for w in range(10)]
        modal = []
        for k in range(10):
            total = coef[0, k] * section[0]
            for w in range(1, 10):
                total = total + coef[w, k] * section[w]
            modal.append(total / (dcol[at, :] + wval[k]))
        for w in range(10):
            total = coef[w, 0] * modal[0]
            for k in range(1, 10):
                total = total + coef[w, k] * modal[k]
            half[at, tile_of(w)] = total
        return 0

    lax.fori_loop(0, 13, rows, 0)
    boxes[0:96, :] = jnp.dot(
        mat_t[0:96, :], half[...], precision=HIGHEST, preferred_element_type=F32
    )


def return_planes(boxes, planes):
    for p, first in enumerate((72, 64, 88, 80)):
        for k in range(8):
            planes[p, pl.ds(k, 8, stride=8), :] = boxes[first : first + 8, tile_of(k + 1)]


def sum_cells(planes, arrived, boxes, sums, out):
    lane = lane_iota(8)
    upper = (lane & 16) != 0
    layer = lane_iota(64) & 15
    for k in range(8):
        value = boxes[0:64, tile_of(k + 1)]
        if k == 7:
            value = value + jnp.where(
                layer == 15, 0.0, pltpu.roll(boxes[0:64, tile_of(0)], 127, 1)
            )
        if k == 0:
            value = value + jnp.where(layer == 0, 0.0, pltpu.roll(boxes[0:64, tile_of(9)], 1, 1))
        sums[k] = value
        at = pl.ds(k, 8, stride=8)
        own, far = planes[0, at, :], arrived[0, at, :]
        sums[k, 0:8, :] += pltpu.roll(jnp.where(lane >= 96, far, own), 32, 1)
        own, far = planes[1, at, :], arrived[1, at, :]
        sums[k, 56:64, :] += pltpu.roll(jnp.where(lane < 32, far, own), 96, 1)
        own, far = planes[2, at, :], arrived[2, at, :]
        sums[k, pl.ds(0, 8, stride=8), :] += jnp.where(
            upper, pltpu.roll(own, 16, 1), pltpu.roll(far, 112, 1)
        )
        own, far = planes[3, at, :], arrived[3, at, :]
        sums[k, pl.ds(7, 8, stride=8), :] += jnp.where(
            upper, pltpu.roll(far, 16, 1), pltpu.roll(own, 112, 1)
        )
    src = lax.broadcasted_iota(jnp.int32, (128, 128), 0)
    to = lax.broadcasted_iota(jnp.int32, (128, 128), 1)
    order = jnp.where(to == (src & 15) * 8 + (src >> 4), 1.0, 0.0)
    group = lane_iota(64) >> 4
    for b in range(8):
        mixed = jnp.zeros((64, 128), F32)
        for k in range(8):
            turned = pltpu.roll(sums[k], ((k - b) % 8) * 16, 1) if k != b else sums[k]
            mixed = jnp.where(group == k, turned, mixed)
        mixed = jnp.dot(mixed, order, precision=HIGHEST, preferred_element_type=F32)
        for i in range(8):
            first = ((b // 2) * 8 + i) * 16 + (b % 2) * 8
            out[first : first + 8, :] = mixed[8 * i : 8 * i + 8, :]


def target_rows(place, idx_v, marks):
    live = place >= 0
    p = jnp.maximum(place, 0)
    layer = p & 15
    es = (p >> 4) & 15
    ex = p >> 8
    target = ((ex >> 2) * 8 + (es >> 1)).astype(F32)
    row = (((ex & 3) * 2 + (es & 1)) * 16 + layer).astype(F32)
    key = jnp.where(live, target, -1.0)
    ri = lax.broadcasted_iota(jnp.int32, (ROWS, ROWS), 0)
    ci = lax.broadcasted_iota(jnp.int32, (ROWS, ROWS), 1)
    rf = ri.astype(F32)
    cf = ci.astype(F32)
    same = ri == ci
    key_b = jnp.broadcast_to(key, (ROWS, ROWS))
    key_c = jnp.sum(jnp.where(same, key_b, 0.0), axis=1, keepdims=True)
    rank = jnp.sum(jnp.where((key_c == key_b) & (ri < ci), 1.0, 0.0), axis=0, keepdims=True)
    pos = jnp.where(live, target * 2.0 + rank, -1.0)
    pos_b = jnp.broadcast_to(pos, (ROWS, ROWS))
    pos_c = jnp.sum(jnp.where(same, pos_b, 0.0), axis=1, keepdims=True)
    idx = jnp.sum(jnp.where(pos_c == cf, rf, 0.0), axis=0, keepdims=True)
    idx_v[...] = idx.astype(jnp.int32)
    row_b = jnp.broadcast_to(row + 1.0, (ROWS, ROWS))
    mark = jnp.sum(jnp.where(pos_b == rf, row_b, 0.0), axis=1, keepdims=True) - 1.0
    marks[...] = jnp.broadcast_to(mark, (ROWS, 128)).reshape(ROWS, 1, 128)


def pack_chunk(idx_s, old, packed):
    def body(step, _):
        for more in range(4):
            r = step * 4 + more
            s = idx_s[0, r] & (ROWS - 1)
            base = (s >> 3) * 32 + (s & 7)
            for f in range(FPC):
                packed[r, 4 * f : 4 * f + 4, :] = old[f, pl.ds(base, 4, stride=8), :]
        return 0

    lax.fori_loop(0, ROWS // 4, body, 0)


def arrived_rows(marks, idx_v):
    rf = lax.broadcasted_iota(jnp.int32, (ROWS, 128), 0).astype(F32)
    nf = lane_iota(ROWS).astype(F32)
    idx = jnp.sum(jnp.where(marks == nf, rf, 0.0), axis=0, keepdims=True)
    idx_v[...] = idx.astype(jnp.int32)


def unpack_chunk(idx_s, recv, stage):
    def body(col, _):
        for layer in range(16):
            a = idx_s[0, col * 16 + layer] & (ROWS - 1)
            start = (layer // 8) * 32 + layer % 8
            for f in range(FPC):
                stage[col, f, pl.ds(start, 4, stride=8), :] = recv[a, 4 * f : 4 * f + 4, :]
        return 0

    lax.fori_loop(0, 8, body, 0)


def whole_kernel(place, old, vx, vs, vw, valx, vals, valw, placed, out, scratch):
    (
        idx_v, idx_s, pos_v, pos_s, marks, marks_in, olds, packs, recvs, stages,
        pad, mat, mat_t, coef, wval, dcol, points, faces, faces_in, boxes, half,
        planes, planes_in, sums, ssem, rsem, msem, hssem, hrsem, osem, wsem, lsem, isem,
    ) = scratch
    gx, gy = my_place()
    me = gx * 8 + gy
    everyone = peers()
    barrier = pltpu.get_barrier_semaphore()
    loads = [
        pltpu.make_async_copy(old.at[pl.ds(FPC * ch, FPC)], olds[ch], osem.at[ch])
        for ch in range(NCH)
    ]
    for copy in loads:
        copy.start()

    def greet(k, _):
        d = lax.rem(me + k, 128)
        pl.semaphore_signal(
            barrier, inc=1, device_id=(d // 8, lax.rem(d, 8)), device_id_type=MESH
        )
        return 0

    lax.fori_loop(1, 128, greet, 0)
    target_rows(place[...], idx_v, marks)
    copy = pltpu.make_async_copy(idx_v, idx_s, isem.at[0])
    copy.start()
    copy.wait()
    own = []

    def pack(ch):
        loads[ch].wait()
        pack_chunk(idx_s, olds[ch], packs[ch])

    def send_one(source, target, send_sem, recv_sem, peer):
        d = peer[0] * 8 + peer[1]
        pltpu.make_async_remote_copy(
            source.at[pl.ds(2 * d, 2)],
            target.at[pl.ds(2 * me, 2)],
            send_sem,
            recv_sem,
            device_id=peer,
            device_id_type=MESH,
        ).start()

    def keep_own(source, target, sem):
        copy = pltpu.make_async_copy(
            source.at[pl.ds(2 * me, 2)], target.at[pl.ds(2 * me, 2)], sem
        )
        copy.start()
        own.append(copy)

    def send(ch):
        for peer in everyone:
            send_one(packs[ch], recvs[ch], ssem.at[ch], rsem.at[ch], peer)
        keep_own(packs[ch], recvs[ch], lsem.at[ch])

    some = pl.ds(0, ROWS - 2)

    def arrive(ch):
        pltpu.make_async_copy(packs[ch].at[some], recvs[ch].at[some], rsem.at[ch]).wait()
        own[ch].wait()

    def unpack(ch):
        unpack_chunk(pos_s, recvs[ch], stages[ch])
        copy = pltpu.make_async_copy(
            stages[ch], placed.at[:, pl.ds(FPC * ch, FPC)], wsem.at[ch]
        )
        copy.start()
        writes.append(copy)

    writes = []
    pack(0)
    pl.semaphore_wait(barrier, 127)
    send(0)
    for peer in everyone:
        send_one(marks, marks_in, msem.at[0], msem.at[1], peer)
    pack(1)
    send(1)
    keep_own(marks, marks_in, lsem.at[NCH])
    pack(2)
    own_marks = own.pop()
    send(2)
    for ch in range(3, NCH):
        pack(ch)
    build_tables(vx, vs, vw, valx, vals, valw, pad, mat, mat_t, coef, wval, dcol)
    pltpu.make_async_copy(marks.at[some], marks_in.at[some], msem.at[1]).wait()
    own_marks.wait()
    marks_here = marks_in[...].reshape(ROWS, 128)
    arrived_rows(marks_here, pos_v)
    copy = pltpu.make_async_copy(pos_v, pos_s, isem.at[1])
    copy.start()
    copy.wait()
    arrive(0)
    arrive(1)
    right_side([recvs[ch].reshape(ROWS * W, 128) for ch in range(2)], marks_here, points)
    gather_planes(points, faces)
    sources = (points.at[pl.ds(448, 64)], points.at[pl.ds(0, 64)], faces.at[0], faces.at[1])
    halo = plane_copies(sources, faces_in, hssem, hrsem, 0)
    for copy in halo:
        copy.start()
    send(3)
    fill_inner(points, boxes)
    unpack(0)
    unpack(1)
    for copy in halo:
        copy.wait()
    fill_faces(points, faces, faces_in, boxes)
    solve_boxes(boxes, half, mat, mat_t, coef, wval, dcol)
    return_planes(boxes, planes)
    halo = plane_copies([planes.at[p] for p in range(4)], planes_in, hssem, hrsem, 4)
    for copy in halo:
        copy.start()
    send(4)
    send(5)
    arrive(2)
    unpack(2)
    for copy in halo:
        copy.wait()
    sum_cells(planes, planes_in, boxes, sums, out)
    for ch in range(3, NCH):
        arrive(ch)
        unpack(ch)
    pltpu.make_async_copy(marks.at[some], marks_in.at[some], msem.at[0]).wait()
    for ch in range(NCH):
        pltpu.make_async_copy(packs[ch].at[some], recvs[ch].at[some], ssem.at[ch]).wait()
    for copy in writes:
        copy.wait()


SCRATCH = (
    pltpu.VMEM((1, ROWS), jnp.int32),
    pltpu.SMEM((1, ROWS), jnp.int32),
    pltpu.VMEM((1, 128), jnp.int32),
    pltpu.SMEM((1, 128), jnp.int32),
    pltpu.VMEM((ROWS, 1, 128), F32),
    pltpu.VMEM((ROWS, 1, 128), F32),
    [pltpu.VMEM((FPC, ROWS * 4, 128), F32)] * NCH,
    [pltpu.VMEM((ROWS, W, 128), F32)] * NCH,
    [pltpu.VMEM((ROWS, W, 128), F32)] * NCH,
    [pltpu.VMEM((8, FPC, 64, 128), F32)] * NCH,
    pltpu.VMEM((16, 128), F32),
    pltpu.VMEM((128, 128), F32),
    pltpu.VMEM((128, 128), F32),
    pltpu.VMEM((10, 10, 8, 128), F32),
    pltpu.VMEM((10, 8, 128), F32),
    pltpu.VMEM((128, 128), F32),
    pltpu.VMEM((512, 128), F32),
    pltpu.VMEM((2, 64, 128), F32),
    pltpu.VMEM((4, 64, 128), F32),
    pltpu.VMEM((128, 1280), F32),
    pltpu.VMEM((128, 1280), F32),
    pltpu.VMEM((4, 64, 128), F32),
    pltpu.VMEM((4, 64, 128), F32),
    pltpu.VMEM((8, 64, 128), F32),
    pltpu.SemaphoreType.DMA((NCH,)),
    pltpu.SemaphoreType.DMA((NCH,)),
    pltpu.SemaphoreType.DMA((2,)),
    pltpu.SemaphoreType.DMA((8,)),
    pltpu.SemaphoreType.DMA((8,)),
    pltpu.SemaphoreType.DMA((NCH,)),
    pltpu.SemaphoreType.DMA((NCH,)),
    pltpu.SemaphoreType.DMA((NCH + 1,)),
    pltpu.SemaphoreType.DMA((2,)),
)


def shards(old_states, new_place, vectors_x, vectors_s, vectors_w, values_x, values_s, values_w):
    old_view = old_states.transpose(1, 0, 2).reshape(FIELDS, 32, 8, 4, 128)
    old_view = old_view.transpose(0, 1, 3, 2, 4).reshape(FIELDS, ROWS * 4, 128)
    vmem = pl.BlockSpec(memory_space=pltpu.VMEM)
    far = pl.BlockSpec(memory_space=pl.ANY)
    placed, correction = pl.pallas_call(
        whole_kernel,
        in_specs=[vmem, far] + [vmem] * 6,
        out_specs=[far, vmem],
        out_shape=[
            jax.ShapeDtypeStruct((8, FIELDS, 64, 128), F32),
            jax.ShapeDtypeStruct((512, 128), F32),
        ],
        scratch_shapes=[SCRATCH],
        compiler_params=pltpu.CompilerParams(collective_id=1, has_side_effects=True),
        name="migrate_and_sweep",
    )(
        new_place.reshape(1, ROWS),
        old_view,
        vectors_x,
        vectors_s,
        vectors_w.transpose(1, 0, 2),
        values_x.reshape(1, 10),
        values_s.reshape(1, 10),
        values_w,
    )
    placed = placed.reshape(4, 2, FIELDS, 2, 4, 8, 128).transpose(0, 1, 3, 5, 2, 4, 6)
    return placed.reshape(4, 2, 16, FIELDS, 512), correction.reshape(32, 16, 128)


def solution(mesh):
    placed = (P(("gx", "gy"), None, None), P(("gx", "gy")), P(), P(), P(), P(), P(), P())
    return jax.shard_map(
        shards,
        mesh=mesh,
        in_specs=placed,
        out_specs=(P("gx", "gy", None, None, None), P("gx", "gy", None)),
        check_vma=False,
    )
```

```python
import functools
import jax
import jax.numpy as jnp
from jax import lax
from jax.experimental import pallas as pl
from jax.experimental.pallas import tpu as pltpu
from jax.sharding import PartitionSpec as P

MESH = pl.DeviceIdType.MESH
HIGHEST = lax.Precision.HIGHEST
F32 = jnp.float32

FIELDS = 12
FPC = 2
NCH = FIELDS // FPC
W = 4 * FPC
ROWS = 256


def send_order():
    left = [
        (a, b, c) for a in range(4) for b in range(4) for c in range(4) if (a, b, c) != (0, 0, 0)
    ]
    load = [0] * 6
    order = []

    def with_step(step):
        out = list(load)
        for axis, value in enumerate(step):
            if value in (1, 2):
                out[2 * axis] += 1
            if value in (2, 3):
                out[2 * axis + 1] += 1
        return out

    def cost(step):
        after = with_step(step)
        total = sum(after)
        return (6 * max(after) - total, sum(v * v for v in after) * 6 - total * total, step)

    while left:
        best = min(left, key=cost)
        left.remove(best)
        load[:] = with_step(best)
        order.append(best)
    return order


ORDER = send_order()
LAST = sorted(ORDER, key=lambda step: -sum(min(v, 4 - v) for v in step))


def my_place():
    gx = lax.axis_index("gx")
    gy = lax.axis_index("gy")
    return gx, gy


def peers(steps):
    gx, gy = my_place()
    x, z = gx // 4, lax.rem(gx, 4)
    y, core = gy // 2, lax.rem(gy, 2)
    other = 1 - core
    out = [(gx, y * 2 + other)]
    pairs = [(to, step) for to in (core, other) for step in steps]
    if steps is LAST:
        pairs = [(to, step) for step in steps for to in (core, other)]
    for to_core, step in pairs:
        if True:
            hop = [step[i] * (1 - core) + (4 - step[i]) * core for i in range(3)]
            px = lax.rem(x + hop[0], 4)
            py = lax.rem(y + hop[1], 4)
            pz = lax.rem(z + hop[2], 4)
            out.append((px * 4 + pz, py * 2 + to_core))
    return out


def lane_iota(rows):
    return lax.broadcasted_iota(jnp.int32, (rows, 128), 1)


def tile_of(k):
    return slice(k * 128, (k + 1) * 128)


def build_tables(vx, vs, vw, valx, vals, valw, pad, mat, mat_t, coef, wval, dcol):
    q = lax.broadcasted_iota(jnp.int32, (16, 128), 1)
    u_row = lax.broadcasted_iota(jnp.int32, (16, 128), 0)
    along = (q & 7) + 1
    u_of = jnp.where(q < 64, (q >> 3) + 1, jnp.where(q < 72, 0, jnp.where(q < 80, 9, along)))
    v_of = jnp.where(q < 80, along, jnp.where(q < 88, 0, 9))
    pick_u = jnp.where((u_row == u_of) & (q < 96), 1.0, 0.0)
    pick_v = jnp.where((u_row == v_of) & (q < 96), 1.0, 0.0)
    big_r = lax.broadcasted_iota(jnp.int32, (128, 128), 0)
    big_c = lax.broadcasted_iota(jnp.int32, (128, 128), 1)
    i_of = (big_r * 205) >> 11
    j_of = big_r - i_of * 10
    pick_i = jnp.where((big_c == i_of) & (big_r < 100), 1.0, 0.0)
    pick_j = jnp.where((big_c == j_of) & (big_r < 100), 1.0, 0.0)
    first = (((0,), (0,)), ((), ()))

    def padded(value, width=10):
        pad[...] = jnp.zeros((16, 128), F32)
        pad[0 : value.shape[0], 0:width] = value
        return pad[...]

    def grow(vec, pick_q, pick_row):
        side = lax.dot_general(
            padded(vec), pick_q, first, precision=HIGHEST, preferred_element_type=F32
        )
        return jnp.dot(pick_row, side, precision=HIGHEST, preferred_element_type=F32)

    both = grow(vx[...], pick_u, pick_i) * grow(vs[...], pick_v, pick_j)
    mat[...] = both
    mat_t[...] = both.T
    rows = padded(valx[...])[0:1, :]
    d = jnp.sum(pick_i * rows, axis=1, keepdims=True)
    rows = padded(vals[...])[0:1, :]
    d = d + jnp.sum(pick_j * rows, axis=1, keepdims=True)
    dcol[...] = jnp.broadcast_to(d, (128, 128))
    spread = jnp.where(u_row == (q & 15), 1.0, 0.0)
    for w in range(10):
        table = lax.dot_general(
            padded(vw[w]), spread, first, precision=HIGHEST, preferred_element_type=F32
        )
        for k in range(10):
            coef[w, k] = jnp.broadcast_to(table[k : k + 1, :], (8, 128))
    table = lax.dot_general(
        padded(valw[...]), spread, first, precision=HIGHEST, preferred_element_type=F32
    )
    for k in range(10):
        wval[k] = jnp.broadcast_to(table[k : k + 1, :], (8, 128))


def right_side(arrived, marks, points):
    nf = lane_iota(ROWS).astype(F32)
    chosen = jnp.where(marks == nf, 1.0, 0.0)
    for c in range(4):
        f0, f1, f2 = (
            arrived[f // FPC][pl.ds(4 * (f % FPC) + c, ROWS, stride=W), :] for f in range(3)
        )
        rows = 3.0 * f0 - 3.0 * f1 + f2
        points[128 * c : 128 * (c + 1), :] = jnp.dot(
            rows.T, chosen, precision=HIGHEST, preferred_element_type=F32
        )


def gather_planes(points, planes):
    for i in range(8):
        planes[0, 8 * i : 8 * i + 8, :] = points[64 * i + 56 : 64 * i + 64, :]
        planes[1, 8 * i : 8 * i + 8, :] = points[64 * i : 64 * i + 8, :]


def neighbours():
    gx, gy = my_place()
    return (
        (lax.rem(gx + 1, 16), gy),
        (lax.rem(gx + 15, 16), gy),
        (gx, lax.rem(gy + 1, 8)),
        (gx, lax.rem(gy + 7, 8)),
    )


def plane_copies(sources, target, ssem, rsem, base):
    return [
        pltpu.make_async_remote_copy(
            sources[p],
            target.at[p],
            ssem.at[base + p],
            rsem.at[base + p],
            device_id=peer,
            device_id_type=MESH,
        )
        for p, peer in enumerate(neighbours())
    ]


def fill_inner(points, boxes):
    boxes[96:128, :] = jnp.zeros((32, 1280), F32)
    boxes[64:96, tile_of(0)] = jnp.zeros((32, 128), F32)
    boxes[64:96, tile_of(9)] = jnp.zeros((32, 128), F32)
    layer = lane_iota(64) & 15
    for k in range(8):
        value = points[pl.ds(k, 64, stride=8), :]
        boxes[0:64, tile_of(k + 1)] = value
        if k == 7:
            boxes[0:64, tile_of(0)] = jnp.where(layer == 0, 0.0, pltpu.roll(value, 1, 1))
        if k == 0:
            boxes[0:64, tile_of(9)] = jnp.where(layer == 15, 0.0, pltpu.roll(value, 127, 1))


def fill_faces(points, planes, arrived, boxes):
    lane = lane_iota(8)
    upper = (lane & 16) != 0
    for k in range(8):
        own = points[pl.ds(448 + k, 8, stride=8), :]
        far = arrived[0, pl.ds(k, 8, stride=8), :]
        boxes[64:72, tile_of(k + 1)] = pltpu.roll(jnp.where(lane >= 96, far, own), 32, 1)
        own = points[pl.ds(k, 8, stride=8), :]
        far = arrived[1, pl.ds(k, 8, stride=8), :]
        boxes[72:80, tile_of(k + 1)] = pltpu.roll(jnp.where(lane < 32, far, own), 96, 1)
        own = planes[0, pl.ds(k, 8, stride=8), :]
        far = arrived[2, pl.ds(k, 8, stride=8), :]
        boxes[80:88, tile_of(k + 1)] = jnp.where(
            upper, pltpu.roll(own, 16, 1), pltpu.roll(far, 112, 1)
        )
        own = planes[1, pl.ds(k, 8, stride=8), :]
        far = arrived[3, pl.ds(k, 8, stride=8), :]
        boxes[88:96, tile_of(k + 1)] = jnp.where(
            upper, pltpu.roll(far, 16, 1), pltpu.roll(own, 112, 1)
        )


def solve_boxes(boxes, half, mat, mat_t, coef, wval, dcol):
    half[0:104, :] = jnp.dot(
        mat[0:104, :], boxes[...], precision=HIGHEST, preferred_element_type=F32
    )
    half[104:128, :] = jnp.zeros((24, 1280), F32)

    def rows(t, _):
        at = pl.ds(pl.multiple_of(t * 8, 8), 8)
        section = [half[at, tile_of(w)] for w in range(10)]
        modal = []
        for k in range(10):
            total = coef[0, k] * section[0]
            for w in range(1, 10):
                total = total + coef[w, k] * section[w]
            modal.append(total / (dcol[at, :] + wval[k]))
        for w in range(10):
            total = coef[w, 0] * modal[0]
            for k in range(1, 10):
                total = total + coef[w, k] * modal[k]
            half[at, tile_of(w)] = total
        return 0

    lax.fori_loop(0, 13, rows, 0)
    boxes[0:96, :] = jnp.dot(
        mat_t[0:96, :], half[...], precision=HIGHEST, preferred_element_type=F32
    )


def return_planes(boxes, planes):
    for p, first in enumerate((72, 64, 88, 80)):
        for k in range(8):
            planes[p, pl.ds(k, 8, stride=8), :] = boxes[first : first + 8, tile_of(k + 1)]


def sum_cells(planes, arrived, boxes, sums, out):
    lane = lane_iota(8)
    upper = (lane & 16) != 0
    layer = lane_iota(64) & 15
    for k in range(8):
        value = boxes[0:64, tile_of(k + 1)]
        if k == 7:
            value = value + jnp.where(
                layer == 15, 0.0, pltpu.roll(boxes[0:64, tile_of(0)], 127, 1)
            )
        if k == 0:
            value = value + jnp.where(layer == 0, 0.0, pltpu.roll(boxes[0:64, tile_of(9)], 1, 1))
        sums[k] = value
        at = pl.ds(k, 8, stride=8)
        own, far = planes[0, at, :], arrived[0, at, :]
        sums[k, 0:8, :] += pltpu.roll(jnp.where(lane >= 96, far, own), 32, 1)
        own, far = planes[1, at, :], arrived[1, at, :]
        sums[k, 56:64, :] += pltpu.roll(jnp.where(lane < 32, far, own), 96, 1)
        own, far = planes[2, at, :], arrived[2, at, :]
        sums[k, pl.ds(0, 8, stride=8), :] += jnp.where(
            upper, pltpu.roll(own, 16, 1), pltpu.roll(far, 112, 1)
        )
        own, far = planes[3, at, :], arrived[3, at, :]
        sums[k, pl.ds(7, 8, stride=8), :] += jnp.where(
            upper, pltpu.roll(far, 16, 1), pltpu.roll(own, 112, 1)
        )
    src = lax.broadcasted_iota(jnp.int32, (128, 128), 0)
    to = lax.broadcasted_iota(jnp.int32, (128, 128), 1)
    order = jnp.where(to == (src & 15) * 8 + (src >> 4), 1.0, 0.0)
    group = lane_iota(64) >> 4
    for b in range(8):
        mixed = jnp.zeros((64, 128), F32)
        for k in range(8):
            turned = pltpu.roll(sums[k], ((k - b) % 8) * 16, 1) if k != b else sums[k]
            mixed = jnp.where(group == k, turned, mixed)
        mixed = jnp.dot(mixed, order, precision=HIGHEST, preferred_element_type=F32)
        for i in range(8):
            first = ((b // 2) * 8 + i) * 16 + (b % 2) * 8
            out[first : first + 8, :] = mixed[8 * i : 8 * i + 8, :]


def target_rows(place, idx_v, marks):
    live = place >= 0
    p = jnp.maximum(place, 0)
    layer = p & 15
    es = (p >> 4) & 15
    ex = p >> 8
    target = ((ex >> 2) * 8 + (es >> 1)).astype(F32)
    row = (((ex & 3) * 2 + (es & 1)) * 16 + layer).astype(F32)
    key = jnp.where(live, target, -1.0)
    ri = lax.broadcasted_iota(jnp.int32, (ROWS, ROWS), 0)
    ci = lax.broadcasted_iota(jnp.int32, (ROWS, ROWS), 1)
    rf = ri.astype(F32)
    cf = ci.astype(F32)
    same = ri == ci
    key_b = jnp.broadcast_to(key, (ROWS, ROWS))
    key_c = jnp.sum(jnp.where(same, key_b, 0.0), axis=1, keepdims=True)
    rank = jnp.sum(jnp.where((key_c == key_b) & (ri < ci), 1.0, 0.0), axis=0, keepdims=True)
    pos = jnp.where(live, target * 2.0 + rank, -1.0)
    pos_b = jnp.broadcast_to(pos, (ROWS, ROWS))
    pos_c = jnp.sum(jnp.where(same, pos_b, 0.0), axis=1, keepdims=True)
    idx = jnp.sum(jnp.where(pos_c == cf, rf, 0.0), axis=0, keepdims=True)
    idx_v[...] = idx.astype(jnp.int32)
    row_b = jnp.broadcast_to(row + 1.0, (ROWS, ROWS))
    mark = jnp.sum(jnp.where(pos_b == rf, row_b, 0.0), axis=1, keepdims=True) - 1.0
    marks[...] = jnp.broadcast_to(mark, (ROWS, 128)).reshape(ROWS, 1, 128)


def pack_chunk(idx_s, old, packed):
    def body(step, _):
        for more in range(4):
            r = step * 4 + more
            s = idx_s[0, r] & (ROWS - 1)
            base = (s >> 3) * 32 + (s & 7)
            for f in range(FPC):
                packed[r, 4 * f : 4 * f + 4, :] = old[f, pl.ds(base, 4, stride=8), :]
        return 0

    lax.fori_loop(0, ROWS // 4, body, 0)


def arrived_rows(marks, idx_v):
    rf = lax.broadcasted_iota(jnp.int32, (ROWS, 128), 0).astype(F32)
    nf = lane_iota(ROWS).astype(F32)
    idx = jnp.sum(jnp.where(marks == nf, rf, 0.0), axis=0, keepdims=True)
    idx_v[...] = idx.astype(jnp.int32)


def unpack_chunk(idx_s, recv, placed, first):
    def body(col, _):
        for layer in range(16):
            a = idx_s[0, col * 16 + layer] & (ROWS - 1)
            start = (layer // 8) * 32 + layer % 8
            for f in range(FPC):
                placed[col, first + f, pl.ds(start, 4, stride=8), :] = recv[
                    a, 4 * f : 4 * f + 4, :
                ]
        return 0

    lax.fori_loop(0, 8, body, 0)


def whole_kernel(place, old, vx, vs, vw, valx, vals, valw, placed, out, scratch):
    (
        idx_v, idx_s, pos_v, pos_s, marks, marks_in, olds, packs, recvs,
        pad, mat, mat_t, coef, wval, dcol, points, faces, faces_in, boxes, half,
        planes, planes_in, sums, ssem, rsem, msem, hssem, hrsem, osem, lsem, isem,
    ) = scratch
    gx, gy = my_place()
    me = gx * 8 + gy
    everyone = peers(ORDER)
    last = peers(LAST)
    last = last[1:] + last[:1]
    barrier = pltpu.get_barrier_semaphore()
    loads = [
        pltpu.make_async_copy(old.at[pl.ds(FPC * ch, FPC)], olds[ch], osem.at[ch])
        for ch in range(NCH)
    ]
    for copy in loads:
        copy.start()

    def greet(k, _):
        d = lax.rem(me + k, 128)
        pl.semaphore_signal(
            barrier, inc=1, device_id=(d // 8, lax.rem(d, 8)), device_id_type=MESH
        )
        return 0

    lax.fori_loop(1, 128, greet, 0)
    target_rows(place[...], idx_v, marks)
    copy = pltpu.make_async_copy(idx_v, idx_s, isem.at[0])
    copy.start()
    copy.wait()
    own = []

    def pack(ch):
        loads[ch].wait()
        pack_chunk(idx_s, olds[ch], packs[ch])

    def send_one(source, target, send_sem, recv_sem, peer):
        d = peer[0] * 8 + peer[1]
        pltpu.make_async_remote_copy(
            source.at[pl.ds(2 * d, 2)],
            target.at[pl.ds(2 * me, 2)],
            send_sem,
            recv_sem,
            device_id=peer,
            device_id_type=MESH,
        ).start()

    def keep_own(source, target, sem):
        copy = pltpu.make_async_copy(
            source.at[pl.ds(2 * me, 2)], target.at[pl.ds(2 * me, 2)], sem
        )
        copy.start()
        own.append(copy)

    def send(ch):
        for peer in everyone if ch < NCH - 1 else last:
            send_one(packs[ch], recvs[ch], ssem.at[ch], rsem.at[ch], peer)
        keep_own(packs[ch], recvs[ch], lsem.at[ch])

    some = pl.ds(0, ROWS - 2)

    def arrive(ch):
        pltpu.make_async_copy(packs[ch].at[some], recvs[ch].at[some], rsem.at[ch]).wait()
        own[ch].wait()

    def unpack(ch):
        unpack_chunk(pos_s, recvs[ch], placed, FPC * ch)

    pack(0)
    pl.semaphore_wait(barrier, 127)
    send(0)
    for peer in everyone:
        send_one(marks, marks_in, msem.at[0], msem.at[1], peer)
    pack(1)
    send(1)
    keep_own(marks, marks_in, lsem.at[NCH])
    pack(2)
    own_marks = own.pop()
    send(2)
    for ch in range(3, NCH):
        pack(ch)
    build_tables(vx, vs, vw, valx, vals, valw, pad, mat, mat_t, coef, wval, dcol)
    pltpu.make_async_copy(marks.at[some], marks_in.at[some], msem.at[1]).wait()
    own_marks.wait()
    marks_here = marks_in[...].reshape(ROWS, 128)
    arrived_rows(marks_here, pos_v)
    copy = pltpu.make_async_copy(pos_v, pos_s, isem.at[1])
    copy.start()
    copy.wait()
    arrive(0)
    arrive(1)
    right_side([recvs[ch].reshape(ROWS * W, 128) for ch in range(2)], marks_here, points)
    gather_planes(points, faces)
    sources = (points.at[pl.ds(448, 64)], points.at[pl.ds(0, 64)], faces.at[0], faces.at[1])
    halo = plane_copies(sources, faces_in, hssem, hrsem, 0)
    for copy in halo:
        copy.start()
    send(3)
    fill_inner(points, boxes)
    unpack(0)
    unpack(1)
    for copy in halo:
        copy.wait()
    fill_faces(points, faces, faces_in, boxes)
    solve_boxes(boxes, half, mat, mat_t, coef, wval, dcol)
    return_planes(boxes, planes)
    halo = plane_copies([planes.at[p] for p in range(4)], planes_in, hssem, hrsem, 4)
    for copy in halo:
        copy.start()
    send(4)
    send(5)
    arrive(2)
    unpack(2)
    for copy in halo:
        copy.wait()
    sum_cells(planes, planes_in, boxes, sums, out)
    for ch in range(3, NCH):
        arrive(ch)
        unpack(ch)
    pltpu.make_async_copy(marks.at[some], marks_in.at[some], msem.at[0]).wait()
    for ch in range(NCH):
        pltpu.make_async_copy(packs[ch].at[some], recvs[ch].at[some], ssem.at[ch]).wait()


SCRATCH = (
    pltpu.VMEM((1, ROWS), jnp.int32),
    pltpu.SMEM((1, ROWS), jnp.int32),
    pltpu.VMEM((1, 128), jnp.int32),
    pltpu.SMEM((1, 128), jnp.int32),
    pltpu.VMEM((ROWS, 1, 128), F32),
    pltpu.VMEM((ROWS, 1, 128), F32),
    [pltpu.VMEM((FPC, ROWS * 4, 128), F32)] * NCH,
    [pltpu.VMEM((ROWS, W, 128), F32)] * NCH,
    [pltpu.VMEM((ROWS, W, 128), F32)] * NCH,
    pltpu.VMEM((16, 128), F32),
    pltpu.VMEM((128, 128), F32),
    pltpu.VMEM((128, 128), F32),
    pltpu.VMEM((10, 10, 8, 128), F32),
    pltpu.VMEM((10, 8, 128), F32),
    pltpu.VMEM((128, 128), F32),
    pltpu.VMEM((512, 128), F32),
    pltpu.VMEM((2, 64, 128), F32),
    pltpu.VMEM((4, 64, 128), F32),
    pltpu.VMEM((128, 1280), F32),
    pltpu.VMEM((128, 1280), F32),
    pltpu.VMEM((4, 64, 128), F32),
    pltpu.VMEM((4, 64, 128), F32),
    pltpu.VMEM((8, 64, 128), F32),
    pltpu.SemaphoreType.DMA((NCH,)),
    pltpu.SemaphoreType.DMA((NCH,)),
    pltpu.SemaphoreType.DMA((2,)),
    pltpu.SemaphoreType.DMA((8,)),
    pltpu.SemaphoreType.DMA((8,)),
    pltpu.SemaphoreType.DMA((NCH,)),
    pltpu.SemaphoreType.DMA((NCH + 1,)),
    pltpu.SemaphoreType.DMA((2,)),
)


def shards(old_states, new_place, vectors_x, vectors_s, vectors_w, values_x, values_s, values_w):
    old_view = old_states.transpose(1, 0, 2).reshape(FIELDS, 32, 8, 4, 128)
    old_view = old_view.transpose(0, 1, 3, 2, 4).reshape(FIELDS, ROWS * 4, 128)
    vmem = pl.BlockSpec(memory_space=pltpu.VMEM)
    far = pl.BlockSpec(memory_space=pl.ANY)
    placed, correction = pl.pallas_call(
        whole_kernel,
        in_specs=[vmem, far] + [vmem] * 6,
        out_specs=[vmem, vmem],
        out_shape=[
            pltpu.VMEM((8, FIELDS, 64, 128), F32),
            pltpu.VMEM((512, 128), F32),
        ],
        scratch_shapes=[SCRATCH],
        compiler_params=pltpu.CompilerParams(collective_id=1, has_side_effects=True),
        name="migrate_and_sweep",
    )(
        new_place.reshape(1, ROWS),
        old_view,
        vectors_x,
        vectors_s,
        vectors_w.transpose(1, 0, 2),
        values_x.reshape(1, 10),
        values_s.reshape(1, 10),
        values_w,
    )
    placed = placed.reshape(4, 2, FIELDS, 2, 4, 8, 128).transpose(0, 1, 3, 5, 2, 4, 6)
    return placed.reshape(4, 2, 16, FIELDS, 512), correction.reshape(32, 16, 128)


def solution(mesh):
    placed = (P(("gx", "gy"), None, None), P(("gx", "gy")), P(), P(), P(), P(), P(), P())
    return jax.shard_map(
        shards,
        mesh=mesh,
        in_specs=placed,
        out_specs=(P("gx", "gy", None, None, None), P("gx", "gy", None)),
        check_vma=False,
    )
```

```python
import functools
import jax
import jax.numpy as jnp
from jax import lax
from jax.experimental import pallas as pl
from jax.experimental.pallas import tpu as pltpu
from jax.sharding import PartitionSpec as P

MESH = pl.DeviceIdType.MESH
HIGHEST = lax.Precision.HIGHEST
F32 = jnp.float32

FIELDS = 12
FPC = 2
NCH = FIELDS // FPC
W = 4 * FPC
VMEM_LIMIT = 61_000_000
ROWS = 256


def send_order():
    left = [
        (a, b, c) for a in range(4) for b in range(4) for c in range(4) if (a, b, c) != (0, 0, 0)
    ]
    load = [0] * 6
    order = []

    def with_step(step):
        out = list(load)
        for axis, value in enumerate(step):
            if value in (1, 2):
                out[2 * axis] += 1
            if value in (2, 3):
                out[2 * axis + 1] += 1
        return out

    def cost(step):
        after = with_step(step)
        total = sum(after)
        return (6 * max(after) - total, sum(v * v for v in after) * 6 - total * total, step)

    while left:
        best = min(left, key=cost)
        left.remove(best)
        load[:] = with_step(best)
        order.append(best)
    return order


ORDER = send_order()
LAST = sorted(ORDER, key=lambda step: -sum(min(v, 4 - v) for v in step))


def my_place():
    gx = lax.axis_index("gx")
    gy = lax.axis_index("gy")
    return gx, gy


def peers(steps):
    gx, gy = my_place()
    x, z = gx // 4, lax.rem(gx, 4)
    y, core = gy // 2, lax.rem(gy, 2)
    other = 1 - core
    out = [(gx, y * 2 + other)]
    pairs = [(to, step) for to in (core, other) for step in steps]
    if steps is LAST:
        pairs = [(to, step) for step in steps for to in (core, other)]
    for to_core, step in pairs:
        if True:
            hop = [step[i] * (1 - core) + (4 - step[i]) * core for i in range(3)]
            px = lax.rem(x + hop[0], 4)
            py = lax.rem(y + hop[1], 4)
            pz = lax.rem(z + hop[2], 4)
            out.append((px * 4 + pz, py * 2 + to_core))
    return out


def lane_iota(rows):
    return lax.broadcasted_iota(jnp.int32, (rows, 128), 1)


def tile_of(k):
    return slice(k * 128, (k + 1) * 128)


def build_tables(vx, vs, vw, valx, vals, valw, pad, mat, mat_t, coef, wval, dcol):
    q = lax.broadcasted_iota(jnp.int32, (16, 128), 1)
    u_row = lax.broadcasted_iota(jnp.int32, (16, 128), 0)
    along = (q & 7) + 1
    u_of = jnp.where(q < 64, (q >> 3) + 1, jnp.where(q < 72, 0, jnp.where(q < 80, 9, along)))
    v_of = jnp.where(q < 80, along, jnp.where(q < 88, 0, 9))
    pick_u = jnp.where((u_row == u_of) & (q < 96), 1.0, 0.0)
    pick_v = jnp.where((u_row == v_of) & (q < 96), 1.0, 0.0)
    big_r = lax.broadcasted_iota(jnp.int32, (128, 128), 0)
    big_c = lax.broadcasted_iota(jnp.int32, (128, 128), 1)
    i_of = (big_r * 205) >> 11
    j_of = big_r - i_of * 10
    pick_i = jnp.where((big_c == i_of) & (big_r < 100), 1.0, 0.0)
    pick_j = jnp.where((big_c == j_of) & (big_r < 100), 1.0, 0.0)
    first = (((0,), (0,)), ((), ()))

    def padded(value, width=10):
        pad[...] = jnp.zeros((16, 128), F32)
        pad[0 : value.shape[0], 0:width] = value
        return pad[...]

    def grow(vec, pick_q, pick_row):
        side = lax.dot_general(
            padded(vec), pick_q, first, precision=HIGHEST, preferred_element_type=F32
        )
        return jnp.dot(pick_row, side, precision=HIGHEST, preferred_element_type=F32)

    both = grow(vx[...], pick_u, pick_i) * grow(vs[...], pick_v, pick_j)
    mat[...] = both
    mat_t[...] = both.T
    rows = padded(valx[...])[0:1, :]
    d = jnp.sum(pick_i * rows, axis=1, keepdims=True)
    rows = padded(vals[...])[0:1, :]
    d = d + jnp.sum(pick_j * rows, axis=1, keepdims=True)
    dcol[...] = jnp.broadcast_to(d, (128, 128))
    spread = jnp.where(u_row == (q & 15), 1.0, 0.0)
    for w in range(10):
        table = lax.dot_general(
            padded(vw[w]), spread, first, precision=HIGHEST, preferred_element_type=F32
        )
        for k in range(10):
            coef[w, k] = jnp.broadcast_to(table[k : k + 1, :], (8, 128))
    table = lax.dot_general(
        padded(valw[...]), spread, first, precision=HIGHEST, preferred_element_type=F32
    )
    for k in range(10):
        wval[k] = jnp.broadcast_to(table[k : k + 1, :], (8, 128))


def right_side(arrived, marks, points):
    nf = lane_iota(128).astype(F32)
    chosen = [jnp.where(mark == nf, 1.0, 0.0) for mark in split_marks(marks)]
    for c in range(4):
        total = None
        for slot in range(2):
            f0, f1, f2 = (
                arrived[f // FPC][
                    pl.ds(slot * W + 4 * (f % FPC) + c, 128, stride=2 * W), :
                ]
                for f in range(3)
            )
            rows = 3.0 * f0 - 3.0 * f1 + f2
            part = jnp.dot(
                rows.T, chosen[slot], precision=HIGHEST, preferred_element_type=F32
            )
            total = part if total is None else total + part
        points[128 * c : 128 * (c + 1), :] = total


def gather_planes(points, planes):
    for i in range(8):
        planes[0, 8 * i : 8 * i + 8, :] = points[64 * i + 56 : 64 * i + 64, :]
        planes[1, 8 * i : 8 * i + 8, :] = points[64 * i : 64 * i + 8, :]


def neighbours():
    gx, gy = my_place()
    return (
        (lax.rem(gx + 1, 16), gy),
        (lax.rem(gx + 15, 16), gy),
        (gx, lax.rem(gy + 1, 8)),
        (gx, lax.rem(gy + 7, 8)),
    )


def squeeze_plane(p, read, wire):
    lane = lane_iota(16)
    if p < 2:
        first = 96 if p == 0 else 0
        total = None
        for q in range(4):
            turn = (32 * q - first) % 128
            rows = read(16 * q, 16)
            rows = pltpu.roll(rows, turn, 1) if turn else rows
            total = rows if q == 0 else jnp.where((lane >> 5) == q, rows, total)
        wire[...] = total
    else:
        upper = (lane & 16) != 0
        for half in range(2):
            near, moved = read(16 * half, 16), read(32 + 16 * half, 16)
            moved = pltpu.roll(moved, 112 if p == 2 else 16, 1)
            keep = upper if p == 2 else ~upper
            wire[16 * half : 16 * half + 16, :] = jnp.where(keep, near, moved)


def widen_plane(p, wire, plane):
    if p < 2:
        first = 96 if p == 0 else 0
        for q in range(4):
            turn = (first - 32 * q) % 128
            rows = pltpu.roll(wire[...], turn, 1) if turn else wire[...]
            plane[p, 16 * q : 16 * q + 16, :] = rows
    else:
        plane[p, 0:32, :] = wire[...]
        plane[p, 32:64, :] = pltpu.roll(wire[...], 16 if p == 2 else 112, 1)


def plane_copies(sources, targets, ssem, rsem, base):
    return [
        pltpu.make_async_remote_copy(
            sources[p],
            targets[p],
            ssem.at[base + p],
            rsem.at[base + p],
            device_id=peer,
            device_id_type=MESH,
        )
        for p, peer in enumerate(neighbours())
    ]


def fill_inner(points, boxes):
    boxes[96:128, :] = jnp.zeros((32, 1280), F32)
    boxes[64:96, tile_of(0)] = jnp.zeros((32, 128), F32)
    boxes[64:96, tile_of(9)] = jnp.zeros((32, 128), F32)
    layer = lane_iota(64) & 15
    for k in range(8):
        value = points[pl.ds(k, 64, stride=8), :]
        boxes[0:64, tile_of(k + 1)] = value
        if k == 7:
            boxes[0:64, tile_of(0)] = jnp.where(layer == 0, 0.0, pltpu.roll(value, 1, 1))
        if k == 0:
            boxes[0:64, tile_of(9)] = jnp.where(layer == 15, 0.0, pltpu.roll(value, 127, 1))


def fill_faces(points, planes, arrived, boxes):
    lane = lane_iota(8)
    upper = (lane & 16) != 0
    for k in range(8):
        own = points[pl.ds(448 + k, 8, stride=8), :]
        far = arrived[0, pl.ds(k, 8, stride=8), :]
        boxes[64:72, tile_of(k + 1)] = pltpu.roll(jnp.where(lane >= 96, far, own), 32, 1)
        own = points[pl.ds(k, 8, stride=8), :]
        far = arrived[1, pl.ds(k, 8, stride=8), :]
        boxes[72:80, tile_of(k + 1)] = pltpu.roll(jnp.where(lane < 32, far, own), 96, 1)
        own = planes[0, pl.ds(k, 8, stride=8), :]
        far = arrived[2, pl.ds(k, 8, stride=8), :]
        boxes[80:88, tile_of(k + 1)] = jnp.where(
            upper, pltpu.roll(own, 16, 1), pltpu.roll(far, 112, 1)
        )
        own = planes[1, pl.ds(k, 8, stride=8), :]
        far = arrived[3, pl.ds(k, 8, stride=8), :]
        boxes[88:96, tile_of(k + 1)] = jnp.where(
            upper, pltpu.roll(far, 16, 1), pltpu.roll(own, 112, 1)
        )


def solve_boxes(boxes, half, mat, mat_t, coef, wval, dcol):
    half[0:104, :] = jnp.dot(
        mat[0:104, :], boxes[...], precision=HIGHEST, preferred_element_type=F32
    )
    half[104:128, :] = jnp.zeros((24, 1280), F32)

    def rows(t, _):
        at = pl.ds(pl.multiple_of(t * 8, 8), 8)
        section = [half[at, tile_of(w)] for w in range(10)]
        modal = []
        for k in range(10):
            total = coef[0, k] * section[0]
            for w in range(1, 10):
                total = total + coef[w, k] * section[w]
            modal.append(total / (dcol[at, :] + wval[k]))
        for w in range(10):
            total = coef[w, 0] * modal[0]
            for k in range(1, 10):
                total = total + coef[w, k] * modal[k]
            half[at, tile_of(w)] = total
        return 0

    lax.fori_loop(0, 13, rows, 0)
    boxes[0:96, :] = jnp.dot(
        mat_t[0:96, :], half[...], precision=HIGHEST, preferred_element_type=F32
    )


def return_planes(boxes, planes):
    for p, first in enumerate((72, 64, 88, 80)):
        for k in range(8):
            planes[p, pl.ds(k, 8, stride=8), :] = boxes[first : first + 8, tile_of(k + 1)]


def sum_cells(planes, arrived, boxes, sums, out):
    lane = lane_iota(8)
    upper = (lane & 16) != 0
    layer = lane_iota(64) & 15
    for k in range(8):
        value = boxes[0:64, tile_of(k + 1)]
        if k == 7:
            value = value + jnp.where(
                layer == 15, 0.0, pltpu.roll(boxes[0:64, tile_of(0)], 127, 1)
            )
        if k == 0:
            value = value + jnp.where(layer == 0, 0.0, pltpu.roll(boxes[0:64, tile_of(9)], 1, 1))
        sums[k] = value
        at = pl.ds(k, 8, stride=8)
        own, far = planes[0, at, :], arrived[0, at, :]
        sums[k, 0:8, :] += pltpu.roll(jnp.where(lane >= 96, far, own), 32, 1)
        own, far = planes[1, at, :], arrived[1, at, :]
        sums[k, 56:64, :] += pltpu.roll(jnp.where(lane < 32, far, own), 96, 1)
        own, far = planes[2, at, :], arrived[2, at, :]
        sums[k, pl.ds(0, 8, stride=8), :] += jnp.where(
            upper, pltpu.roll(own, 16, 1), pltpu.roll(far, 112, 1)
        )
        own, far = planes[3, at, :], arrived[3, at, :]
        sums[k, pl.ds(7, 8, stride=8), :] += jnp.where(
            upper, pltpu.roll(far, 16, 1), pltpu.roll(own, 112, 1)
        )
    src = lax.broadcasted_iota(jnp.int32, (128, 128), 0)
    to = lax.broadcasted_iota(jnp.int32, (128, 128), 1)
    order = jnp.where(to == (src & 15) * 8 + (src >> 4), 1.0, 0.0)
    group = lane_iota(64) >> 4
    for b in range(8):
        mixed = jnp.zeros((64, 128), F32)
        for k in range(8):
            turned = pltpu.roll(sums[k], ((k - b) % 8) * 16, 1) if k != b else sums[k]
            mixed = jnp.where(group == k, turned, mixed)
        mixed = jnp.dot(mixed, order, precision=HIGHEST, preferred_element_type=F32)
        for i in range(8):
            first = ((b // 2) * 8 + i) * 16 + (b % 2) * 8
            out[first : first + 8, :] = mixed[8 * i : 8 * i + 8, :]


def target_rows(place, idx_v, marks):
    live = place >= 0
    p = jnp.maximum(place, 0)
    layer = p & 15
    es = (p >> 4) & 15
    ex = p >> 8
    target = ((ex >> 2) * 8 + (es >> 1)).astype(F32)
    row = (((ex & 3) * 2 + (es & 1)) * 16 + layer).astype(F32)
    key = jnp.where(live, target, -1.0)
    ri = lax.broadcasted_iota(jnp.int32, (ROWS, ROWS), 0)
    ci = lax.broadcasted_iota(jnp.int32, (ROWS, ROWS), 1)
    rf = ri.astype(F32)
    cf = ci.astype(F32)
    same = ri == ci
    key_b = jnp.broadcast_to(key, (ROWS, ROWS))
    key_c = jnp.sum(jnp.where(same, key_b, 0.0), axis=1, keepdims=True)
    rank = jnp.sum(jnp.where((key_c == key_b) & (ri < ci), 1.0, 0.0), axis=0, keepdims=True)
    pos = jnp.where(live, target * 2.0 + rank, -1.0)
    pos_b = jnp.broadcast_to(pos, (ROWS, ROWS))
    pos_c = jnp.sum(jnp.where(same, pos_b, 0.0), axis=1, keepdims=True)
    idx = jnp.sum(jnp.where(pos_c == cf, rf, 0.0), axis=0, keepdims=True)
    idx_v[...] = idx.astype(jnp.int32)
    row_b = jnp.broadcast_to(row + 1.0, (128, ROWS))
    pos_b = jnp.broadcast_to(pos, (128, ROWS))
    even = lax.broadcasted_iota(jnp.int32, (128, ROWS), 0).astype(F32) * 2.0
    mark0 = jnp.sum(jnp.where(pos_b == even, row_b, 0.0), axis=1, keepdims=True) - 1.0
    mark1 = jnp.sum(jnp.where(pos_b == even + 1.0, row_b, 0.0), axis=1, keepdims=True) - 1.0
    both = jnp.where(lane_iota(128) < 64, mark0, mark1)
    marks[...] = both.reshape(128, 1, 128)


def pack_chunk(idx_s, old, packed):
    def body(step, _):
        for more in range(4):
            r = step * 4 + more
            s = idx_s[0, r] & (ROWS - 1)
            base = (s >> 3) * 32 + (s & 7)
            for f in range(FPC):
                packed[r, 4 * f : 4 * f + 4, :] = old[f, pl.ds(base, 4, stride=8), :]
        return 0

    lax.fori_loop(0, ROWS // 4, body, 0)


def split_marks(marks):
    return (
        jnp.broadcast_to(marks[:, 0:1], (128, 128)),
        jnp.broadcast_to(marks[:, 64:65], (128, 128)),
    )


def arrived_rows(marks, idx_v):
    even = lax.broadcasted_iota(jnp.int32, (128, 128), 0).astype(F32) * 2.0
    mark0, mark1 = split_marks(marks)
    nf = lane_iota(128).astype(F32)
    idx = jnp.where(mark0 == nf, even, 0.0) + jnp.where(mark1 == nf, even + 1.0, 0.0)
    idx = jnp.sum(idx, axis=0, keepdims=True)
    idx_v[...] = idx.astype(jnp.int32)


def unpack_chunk(idx_s, recv, placed, first):
    def body(col, _):
        for layer in range(16):
            a = idx_s[0, col * 16 + layer] & (ROWS - 1)
            start = (layer // 8) * 32 + layer % 8
            for f in range(FPC):
                placed[col, first + f, pl.ds(start, 4, stride=8), :] = recv[
                    a, 4 * f : 4 * f + 4, :
                ]
        return 0

    lax.fori_loop(0, 8, body, 0)


def whole_kernel(place, old, vx, vs, vw, valx, vals, valw, placed, out, tail, pos_v, scratch):
    (
        idx_v, idx_s, pos_s, marks, marks_in, olds, packs, recvs,
        pad, mat, mat_t, coef, wval, dcol, points, faces, faces_in, boxes, half,
        planes, planes_in, sums, wires, ssem, rsem, msem, hssem, hrsem, osem, lsem, isem,
    ) = scratch
    recvs = list(recvs) + [tail]
    gx, gy = my_place()
    me = gx * 8 + gy
    everyone = peers(ORDER)
    last = peers(LAST)
    last = last[1:] + last[:1]
    barrier = pltpu.get_barrier_semaphore()
    loads = [
        pltpu.make_async_copy(old.at[pl.ds(FPC * ch, FPC)], olds[ch], osem.at[ch])
        for ch in range(NCH)
    ]

    for peer in last:
        pl.semaphore_signal(barrier, inc=1, device_id=peer, device_id_type=MESH)
    for copy in loads:
        copy.start()
    target_rows(place[...], idx_v, marks)
    copy = pltpu.make_async_copy(idx_v, idx_s, isem.at[0])
    copy.start()
    copy.wait()
    own = []

    def pack(ch):
        loads[ch].wait()
        pack_chunk(idx_s, olds[ch], packs[ch])

    def send_one(source, target, send_sem, recv_sem, peer):
        d = peer[0] * 8 + peer[1]
        pltpu.make_async_remote_copy(
            source.at[pl.ds(2 * d, 2)],
            target.at[pl.ds(2 * me, 2)],
            send_sem,
            recv_sem,
            device_id=peer,
            device_id_type=MESH,
        ).start()

    def send_marks(peer):
        pltpu.make_async_remote_copy(
            marks.at[pl.ds(peer[0] * 8 + peer[1], 1)],
            marks_in.at[pl.ds(me, 1)],
            msem.at[0],
            msem.at[1],
            device_id=peer,
            device_id_type=MESH,
        ).start()

    def keep_own(source, target, sem):
        copy = pltpu.make_async_copy(
            source.at[pl.ds(2 * me, 2)], target.at[pl.ds(2 * me, 2)], sem
        )
        copy.start()
        own.append(copy)

    def send(ch):
        for peer in everyone if ch < NCH - 1 else last:
            send_one(packs[ch], recvs[ch], ssem.at[ch], rsem.at[ch], peer)
        keep_own(packs[ch], recvs[ch], lsem.at[ch])

    some = pl.ds(0, ROWS - 2)

    def arrive(ch):
        pltpu.make_async_copy(packs[ch].at[some], recvs[ch].at[some], rsem.at[ch]).wait()
        own[ch].wait()

    def unpack(ch):
        unpack_chunk(pos_s, recvs[ch], placed, FPC * ch)

    pack(0)
    pl.semaphore_wait(barrier, 127)
    send(0)
    for peer in everyone:
        send_marks(peer)
    pack(1)
    send(1)
    own_marks = pltpu.make_async_copy(
        marks.at[pl.ds(me, 1)], marks_in.at[pl.ds(me, 1)], lsem.at[NCH]
    )
    own_marks.start()
    pack(2)
    send(2)
    for ch in range(3, NCH):
        pack(ch)
    build_tables(vx, vs, vw, valx, vals, valw, pad, mat, mat_t, coef, wval, dcol)
    pltpu.make_async_copy(marks.at[pl.ds(0, 127)], marks_in.at[pl.ds(0, 127)], msem.at[1]).wait()
    own_marks.wait()
    marks_here = marks_in[...].reshape(128, 128)
    arrived_rows(marks_here, pos_v)
    copy = pltpu.make_async_copy(pos_v, pos_s, isem.at[1])
    copy.start()
    copy.wait()
    arrive(0)
    arrive(1)
    right_side([recvs[ch].reshape(ROWS * W, 128) for ch in range(2)], marks_here, points)
    gather_planes(points, faces)
    reads = (
        lambda at, n: points[448 + at : 448 + at + n, :],
        lambda at, n: points[at : at + n, :],
        lambda at, n: faces[0, at : at + n, :],
        lambda at, n: faces[1, at : at + n, :],
    )
    for p in range(4):
        squeeze_plane(p, reads[p], wires[p])
    halo = plane_copies(wires[0:4], wires[4:8], hssem, hrsem, 0)
    for copy in halo:
        copy.start()
    send(3)
    fill_inner(points, boxes)
    unpack(0)
    unpack(1)
    for p, copy in enumerate(halo):
        copy.wait()
        widen_plane(p, wires[4 + p], faces_in)
    fill_faces(points, faces, faces_in, boxes)
    solve_boxes(boxes, half, mat, mat_t, coef, wval, dcol)
    return_planes(boxes, planes)
    for p in range(4):
        squeeze_plane(p, lambda at, n, p=p: planes[p, at : at + n, :], wires[8 + p])
    halo = plane_copies(wires[8:12], wires[12:16], hssem, hrsem, 4)
    for copy in halo:
        copy.start()
    send(4)
    send(5)
    arrive(2)
    unpack(2)
    for p, copy in enumerate(halo):
        copy.wait()
        widen_plane(p, wires[12 + p], planes_in)
    sum_cells(planes, planes_in, boxes, sums, out)
    for ch in range(3, NCH - 1):
        arrive(ch)
        unpack(ch)
    arrive(NCH - 1)
    pltpu.make_async_copy(marks.at[pl.ds(0, 127)], marks_in.at[pl.ds(0, 127)], msem.at[0]).wait()
    for ch in range(NCH):
        pltpu.make_async_copy(packs[ch].at[some], recvs[ch].at[some], ssem.at[ch]).wait()


def publish_kernel(placed, correction, tail, pos_v, new_states, out, stage, pos_s, sems):
    index = pltpu.make_async_copy(pos_v, pos_s, sems.at[17])
    index.start()
    done = FIELDS - FPC
    copies = [
        pltpu.make_async_copy(placed.at[c], new_states.at[c, pl.ds(0, done)], sems.at[c])
        for c in range(8)
    ]
    copies.append(pltpu.make_async_copy(correction, out, sems.at[16]))
    for copy in copies:
        copy.start()
    index.wait()
    unpack_chunk(pos_s, tail, stage, 0)
    for c in range(8):
        copies.append(
            pltpu.make_async_copy(stage.at[c], new_states.at[c, pl.ds(done, FPC)], sems.at[8 + c])
        )
        copies[-1].start()
    for copy in copies:
        copy.wait()


SCRATCH = (
    pltpu.VMEM((1, ROWS), jnp.int32),
    pltpu.SMEM((1, ROWS), jnp.int32),
    pltpu.SMEM((1, 128), jnp.int32),
    pltpu.VMEM((128, 1, 128), F32),
    pltpu.VMEM((128, 1, 128), F32),
    [pltpu.VMEM((FPC, ROWS * 4, 128), F32)] * NCH,
    [pltpu.VMEM((ROWS, W, 128), F32)] * NCH,
    [pltpu.VMEM((ROWS, W, 128), F32)] * (NCH - 1),
    pltpu.VMEM((16, 128), F32),
    pltpu.VMEM((128, 128), F32),
    pltpu.VMEM((128, 128), F32),
    pltpu.VMEM((10, 10, 8, 128), F32),
    pltpu.VMEM((10, 8, 128), F32),
    pltpu.VMEM((128, 128), F32),
    pltpu.VMEM((512, 128), F32),
    pltpu.VMEM((2, 64, 128), F32),
    pltpu.VMEM((4, 64, 128), F32),
    pltpu.VMEM((128, 1280), F32),
    pltpu.VMEM((128, 1280), F32),
    pltpu.VMEM((4, 64, 128), F32),
    pltpu.VMEM((4, 64, 128), F32),
    pltpu.VMEM((8, 64, 128), F32),
    [pltpu.VMEM((rows, 128), F32) for rows in (16, 16, 32, 32) * 4],
    pltpu.SemaphoreType.DMA((NCH,)),
    pltpu.SemaphoreType.DMA((NCH,)),
    pltpu.SemaphoreType.DMA((2,)),
    pltpu.SemaphoreType.DMA((8,)),
    pltpu.SemaphoreType.DMA((8,)),
    pltpu.SemaphoreType.DMA((NCH,)),
    pltpu.SemaphoreType.DMA((NCH + 1,)),
    pltpu.SemaphoreType.DMA((2,)),
)


def shards(old_states, new_place, vectors_x, vectors_s, vectors_w, values_x, values_s, values_w):
    old_view = old_states.transpose(1, 0, 2).reshape(FIELDS, 32, 8, 4, 128)
    old_view = old_view.transpose(0, 1, 3, 2, 4).reshape(FIELDS, ROWS * 4, 128)
    vmem = pl.BlockSpec(memory_space=pltpu.VMEM)
    far = pl.BlockSpec(memory_space=pl.ANY)
    results = pl.pallas_call(
        whole_kernel,
        in_specs=[vmem, far] + [vmem] * 6,
        out_specs=[vmem] * 4,
        out_shape=[
            pltpu.VMEM((8, FIELDS - FPC, 64, 128), F32),
            pltpu.VMEM((512, 128), F32),
            pltpu.VMEM((ROWS, W, 128), F32),
            pltpu.VMEM((1, 128), jnp.int32),
        ],
        scratch_shapes=[SCRATCH],
        compiler_params=pltpu.CompilerParams(
            collective_id=1, has_side_effects=True, vmem_limit_bytes=VMEM_LIMIT
        ),
        name="migrate_and_sweep",
    )(
        new_place.reshape(1, ROWS),
        old_view,
        vectors_x,
        vectors_s,
        vectors_w.transpose(1, 0, 2),
        values_x.reshape(1, 10),
        values_s.reshape(1, 10),
        values_w,
    )
    placed, correction = pl.pallas_call(
        publish_kernel,
        in_specs=[vmem] * 4,
        out_specs=[far] * 2,
        out_shape=[
            jax.ShapeDtypeStruct((8, FIELDS, 64, 128), F32),
            jax.ShapeDtypeStruct((512, 128), F32),
        ],
        scratch_shapes=[
            pltpu.VMEM((8, FPC, 64, 128), F32),
            pltpu.SMEM((1, 128), jnp.int32),
            pltpu.SemaphoreType.DMA((18,)),
        ],
        compiler_params=pltpu.CompilerParams(vmem_limit_bytes=VMEM_LIMIT),
        name="publish",
    )(*(pltpu.with_memory_space_constraint(r, pltpu.VMEM) for r in results))
    placed = placed.reshape(4, 2, FIELDS, 2, 4, 8, 128).transpose(0, 1, 3, 5, 2, 4, 6)
    return placed.reshape(4, 2, 16, FIELDS, 512), correction.reshape(32, 16, 128)


def solution(mesh):
    placed = (P(("gx", "gy"), None, None), P(("gx", "gy")), P(), P(), P(), P(), P(), P())
    return jax.shard_map(
        shards,
        mesh=mesh,
        in_specs=placed,
        out_specs=(P("gx", "gy", None, None, None), P("gx", "gy", None)),
        check_vma=False,
    )
```

```python
import functools
import jax
import jax.numpy as jnp
from jax import lax
from jax.experimental import pallas as pl
from jax.experimental.pallas import tpu as pltpu
from jax.sharding import PartitionSpec as P

MESH = pl.DeviceIdType.MESH
HIGHEST = lax.Precision.HIGHEST
F32 = jnp.float32

FIELDS = 12
FPC = 2
NCH = FIELDS // FPC
W = 4 * FPC
VMEM_LIMIT = 61_000_000
ROWS = 256


def send_order():
    left = [
        (a, b, c) for a in range(4) for b in range(4) for c in range(4) if (a, b, c) != (0, 0, 0)
    ]
    load = [0] * 6
    order = []

    def with_step(step):
        out = list(load)
        for axis, value in enumerate(step):
            if value in (1, 2):
                out[2 * axis] += 1
            if value in (2, 3):
                out[2 * axis + 1] += 1
        return out

    def cost(step):
        after = with_step(step)
        total = sum(after)
        return (6 * max(after) - total, sum(v * v for v in after) * 6 - total * total, step)

    while left:
        best = min(left, key=cost)
        left.remove(best)
        load[:] = with_step(best)
        order.append(best)
    return order


ORDER = send_order()
LAST = sorted(ORDER, key=lambda step: -sum(min(v, 4 - v) for v in step))


def my_place():
    gx = lax.axis_index("gx")
    gy = lax.axis_index("gy")
    return gx, gy


def peers(steps):
    gx, gy = my_place()
    x, z = gx // 4, lax.rem(gx, 4)
    y, core = gy // 2, lax.rem(gy, 2)
    other = 1 - core
    out = [(gx, y * 2 + other)]
    pairs = [(to, step) for to in (core, other) for step in steps]
    if steps is LAST:
        pairs = [(to, step) for step in steps for to in (core, other)]
    for to_core, step in pairs:
        if True:
            hop = [step[i] * (1 - core) + (4 - step[i]) * core for i in range(3)]
            px = lax.rem(x + hop[0], 4)
            py = lax.rem(y + hop[1], 4)
            pz = lax.rem(z + hop[2], 4)
            out.append((px * 4 + pz, py * 2 + to_core))
    return out


def lane_iota(rows):
    return lax.broadcasted_iota(jnp.int32, (rows, 128), 1)


def tile_of(k):
    return slice(k * 128, (k + 1) * 128)


def build_tables(vx, vs, vw, valx, vals, valw, pad, mat, mat_t, coef, wval, dcol):
    q = lax.broadcasted_iota(jnp.int32, (16, 128), 1)
    u_row = lax.broadcasted_iota(jnp.int32, (16, 128), 0)
    along = (q & 7) + 1
    u_of = jnp.where(q < 64, (q >> 3) + 1, jnp.where(q < 72, 0, jnp.where(q < 80, 9, along)))
    v_of = jnp.where(q < 80, along, jnp.where(q < 88, 0, 9))
    pick_u = jnp.where((u_row == u_of) & (q < 96), 1.0, 0.0)
    pick_v = jnp.where((u_row == v_of) & (q < 96), 1.0, 0.0)
    big_r = lax.broadcasted_iota(jnp.int32, (128, 128), 0)
    big_c = lax.broadcasted_iota(jnp.int32, (128, 128), 1)
    i_of = (big_r * 205) >> 11
    j_of = big_r - i_of * 10
    pick_i = jnp.where((big_c == i_of) & (big_r < 100), 1.0, 0.0)
    pick_j = jnp.where((big_c == j_of) & (big_r < 100), 1.0, 0.0)
    first = (((0,), (0,)), ((), ()))

    def padded(value, width=10):
        pad[...] = jnp.zeros((16, 128), F32)
        pad[0 : value.shape[0], 0:width] = value
        return pad[...]

    def grow(vec, pick_q, pick_row):
        side = lax.dot_general(
            padded(vec), pick_q, first, precision=HIGHEST, preferred_element_type=F32
        )
        return jnp.dot(pick_row, side, precision=HIGHEST, preferred_element_type=F32)

    both = grow(vx[...], pick_u, pick_i) * grow(vs[...], pick_v, pick_j)
    mat[...] = both
    mat_t[...] = both.T
    rows = padded(valx[...])[0:1, :]
    d = jnp.sum(pick_i * rows, axis=1, keepdims=True)
    rows = padded(vals[...])[0:1, :]
    d = d + jnp.sum(pick_j * rows, axis=1, keepdims=True)
    dcol[...] = jnp.broadcast_to(d, (128, 128))
    spread = jnp.where(u_row == (q & 15), 1.0, 0.0)
    for w in range(10):
        table = lax.dot_general(
            padded(vw[w]), spread, first, precision=HIGHEST, preferred_element_type=F32
        )
        for k in range(10):
            coef[w, k] = jnp.broadcast_to(table[k : k + 1, :], (8, 128))
    table = lax.dot_general(
        padded(valw[...]), spread, first, precision=HIGHEST, preferred_element_type=F32
    )
    for k in range(10):
        wval[k] = jnp.broadcast_to(table[k : k + 1, :], (8, 128))


def right_side(arrived, marks, points):
    nf = lane_iota(128).astype(F32)
    chosen = [jnp.where(mark == nf, 1.0, 0.0) for mark in split_marks(marks)]
    for c in range(4):
        total = None
        for slot in range(2):
            f0, f1, f2 = (
                arrived[f // FPC][
                    pl.ds(slot * W + 4 * (f % FPC) + c, 128, stride=2 * W), :
                ]
                for f in range(3)
            )
            rows = 3.0 * f0 - 3.0 * f1 + f2
            part = jnp.dot(
                rows.T, chosen[slot], precision=HIGHEST, preferred_element_type=F32
            )
            total = part if total is None else total + part
        points[128 * c : 128 * (c + 1), :] = total


def gather_planes(points, planes):
    for i in range(8):
        planes[0, 8 * i : 8 * i + 8, :] = points[64 * i + 56 : 64 * i + 64, :]
        planes[1, 8 * i : 8 * i + 8, :] = points[64 * i : 64 * i + 8, :]


def neighbours():
    gx, gy = my_place()
    return (
        (lax.rem(gx + 1, 16), gy),
        (lax.rem(gx + 15, 16), gy),
        (gx, lax.rem(gy + 1, 8)),
        (gx, lax.rem(gy + 7, 8)),
    )


def squeeze_plane(p, read, wire):
    lane = lane_iota(16)
    if p < 2:
        first = 96 if p == 0 else 0
        total = None
        for q in range(4):
            turn = (32 * q - first) % 128
            rows = read(16 * q, 16)
            rows = pltpu.roll(rows, turn, 1) if turn else rows
            total = rows if q == 0 else jnp.where((lane >> 5) == q, rows, total)
        wire[...] = total
    else:
        upper = (lane & 16) != 0
        for half in range(2):
            near, moved = read(16 * half, 16), read(32 + 16 * half, 16)
            moved = pltpu.roll(moved, 112 if p == 2 else 16, 1)
            keep = upper if p == 2 else ~upper
            wire[16 * half : 16 * half + 16, :] = jnp.where(keep, near, moved)


def widen_plane(p, wire, plane):
    if p < 2:
        first = 96 if p == 0 else 0
        for q in range(4):
            turn = (first - 32 * q) % 128
            rows = pltpu.roll(wire[...], turn, 1) if turn else wire[...]
            plane[p, 16 * q : 16 * q + 16, :] = rows
    else:
        plane[p, 0:32, :] = wire[...]
        plane[p, 32:64, :] = pltpu.roll(wire[...], 16 if p == 2 else 112, 1)


def plane_copies(sources, targets, ssem, rsem, base):
    return [
        pltpu.make_async_remote_copy(
            sources[p],
            targets[p],
            ssem.at[base + p],
            rsem.at[base + p],
            device_id=peer,
            device_id_type=MESH,
        )
        for p, peer in enumerate(neighbours())
    ]


def fill_inner(points, boxes):
    boxes[96:128, :] = jnp.zeros((32, 1280), F32)
    boxes[64:96, tile_of(0)] = jnp.zeros((32, 128), F32)
    boxes[64:96, tile_of(9)] = jnp.zeros((32, 128), F32)
    layer = lane_iota(64) & 15
    for k in range(8):
        value = points[pl.ds(k, 64, stride=8), :]
        boxes[0:64, tile_of(k + 1)] = value
        if k == 7:
            boxes[0:64, tile_of(0)] = jnp.where(layer == 0, 0.0, pltpu.roll(value, 1, 1))
        if k == 0:
            boxes[0:64, tile_of(9)] = jnp.where(layer == 15, 0.0, pltpu.roll(value, 127, 1))


def fill_faces(points, planes, arrived, boxes):
    lane = lane_iota(8)
    upper = (lane & 16) != 0
    for k in range(8):
        own = points[pl.ds(448 + k, 8, stride=8), :]
        far = arrived[0, pl.ds(k, 8, stride=8), :]
        boxes[64:72, tile_of(k + 1)] = pltpu.roll(jnp.where(lane >= 96, far, own), 32, 1)
        own = points[pl.ds(k, 8, stride=8), :]
        far = arrived[1, pl.ds(k, 8, stride=8), :]
        boxes[72:80, tile_of(k + 1)] = pltpu.roll(jnp.where(lane < 32, far, own), 96, 1)
        own = planes[0, pl.ds(k, 8, stride=8), :]
        far = arrived[2, pl.ds(k, 8, stride=8), :]
        boxes[80:88, tile_of(k + 1)] = jnp.where(
            upper, pltpu.roll(own, 16, 1), pltpu.roll(far, 112, 1)
        )
        own = planes[1, pl.ds(k, 8, stride=8), :]
        far = arrived[3, pl.ds(k, 8, stride=8), :]
        boxes[88:96, tile_of(k + 1)] = jnp.where(
            upper, pltpu.roll(far, 16, 1), pltpu.roll(own, 112, 1)
        )


def solve_boxes(boxes, half, mat, mat_t, coef, wval, dcol):
    half[0:104, :] = jnp.dot(
        mat[0:104, :], boxes[...], precision=HIGHEST, preferred_element_type=F32
    )
    half[104:128, :] = jnp.zeros((24, 1280), F32)

    def rows(t, _):
        at = pl.ds(pl.multiple_of(t * 8, 8), 8)
        section = [half[at, tile_of(w)] for w in range(10)]
        modal = []
        for k in range(10):
            total = coef[0, k] * section[0]
            for w in range(1, 10):
                total = total + coef[w, k] * section[w]
            modal.append(total / (dcol[at, :] + wval[k]))
        for w in range(10):
            total = coef[w, 0] * modal[0]
            for k in range(1, 10):
                total = total + coef[w, k] * modal[k]
            half[at, tile_of(w)] = total
        return 0

    lax.fori_loop(0, 13, rows, 0)
    boxes[0:96, :] = jnp.dot(
        mat_t[0:96, :], half[...], precision=HIGHEST, preferred_element_type=F32
    )


def return_planes(boxes, planes):
    for p, first in enumerate((72, 64, 88, 80)):
        for k in range(8):
            planes[p, pl.ds(k, 8, stride=8), :] = boxes[first : first + 8, tile_of(k + 1)]


def sum_cells(planes, arrived, boxes, sums, out):
    lane = lane_iota(8)
    upper = (lane & 16) != 0
    layer = lane_iota(64) & 15
    for k in range(8):
        value = boxes[0:64, tile_of(k + 1)]
        if k == 7:
            value = value + jnp.where(
                layer == 15, 0.0, pltpu.roll(boxes[0:64, tile_of(0)], 127, 1)
            )
        if k == 0:
            value = value + jnp.where(layer == 0, 0.0, pltpu.roll(boxes[0:64, tile_of(9)], 1, 1))
        sums[k] = value
        at = pl.ds(k, 8, stride=8)
        own, far = planes[0, at, :], arrived[0, at, :]
        sums[k, 0:8, :] += pltpu.roll(jnp.where(lane >= 96, far, own), 32, 1)
        own, far = planes[1, at, :], arrived[1, at, :]
        sums[k, 56:64, :] += pltpu.roll(jnp.where(lane < 32, far, own), 96, 1)
        own, far = planes[2, at, :], arrived[2, at, :]
        sums[k, pl.ds(0, 8, stride=8), :] += jnp.where(
            upper, pltpu.roll(own, 16, 1), pltpu.roll(far, 112, 1)
        )
        own, far = planes[3, at, :], arrived[3, at, :]
        sums[k, pl.ds(7, 8, stride=8), :] += jnp.where(
            upper, pltpu.roll(far, 16, 1), pltpu.roll(own, 112, 1)
        )
    src = lax.broadcasted_iota(jnp.int32, (128, 128), 0)
    to = lax.broadcasted_iota(jnp.int32, (128, 128), 1)
    order = jnp.where(to == (src & 15) * 8 + (src >> 4), 1.0, 0.0)
    group = lane_iota(64) >> 4
    for b in range(8):
        mixed = jnp.zeros((64, 128), F32)
        for k in range(8):
            turned = pltpu.roll(sums[k], ((k - b) % 8) * 16, 1) if k != b else sums[k]
            mixed = jnp.where(group == k, turned, mixed)
        mixed = jnp.dot(mixed, order, precision=HIGHEST, preferred_element_type=F32)
        for i in range(8):
            first = ((b // 2) * 8 + i) * 16 + (b % 2) * 8
            out[first : first + 8, :] = mixed[8 * i : 8 * i + 8, :]


def target_rows(place, idx_v, marks):
    live = place >= 0
    p = jnp.maximum(place, 0)
    layer = p & 15
    es = (p >> 4) & 15
    ex = p >> 8
    target = ((ex >> 2) * 8 + (es >> 1)).astype(F32)
    row = (((ex & 3) * 2 + (es & 1)) * 16 + layer).astype(F32)
    key = jnp.where(live, target, -1.0)
    ri = lax.broadcasted_iota(jnp.int32, (ROWS, ROWS), 0)
    ci = lax.broadcasted_iota(jnp.int32, (ROWS, ROWS), 1)
    rf = ri.astype(F32)
    cf = ci.astype(F32)
    same = ri == ci
    key_b = jnp.broadcast_to(key, (ROWS, ROWS))
    key_c = jnp.sum(jnp.where(same, key_b, 0.0), axis=1, keepdims=True)
    rank = jnp.sum(jnp.where((key_c == key_b) & (ri < ci), 1.0, 0.0), axis=0, keepdims=True)
    pos = jnp.where(live, target * 2.0 + rank, -1.0)
    pos_b = jnp.broadcast_to(pos, (ROWS, ROWS))
    pos_c = jnp.sum(jnp.where(same, pos_b, 0.0), axis=1, keepdims=True)
    idx = jnp.sum(jnp.where(pos_c == cf, rf, 0.0), axis=0, keepdims=True)
    idx_v[...] = idx.astype(jnp.int32)
    row_b = jnp.broadcast_to(row + 1.0, (128, ROWS))
    pos_b = jnp.broadcast_to(pos, (128, ROWS))
    even = lax.broadcasted_iota(jnp.int32, (128, ROWS), 0).astype(F32) * 2.0
    mark0 = jnp.sum(jnp.where(pos_b == even, row_b, 0.0), axis=1, keepdims=True) - 1.0
    mark1 = jnp.sum(jnp.where(pos_b == even + 1.0, row_b, 0.0), axis=1, keepdims=True) - 1.0
    both = jnp.where(lane_iota(128) < 64, mark0, mark1)
    marks[...] = both.reshape(128, 1, 128)


def pack_chunk(idx_s, old, packed):
    def body(step, _):
        for more in range(4):
            r = step * 4 + more
            s = idx_s[0, r] & (ROWS - 1)
            base = (s >> 3) * 32 + (s & 7)
            for f in range(FPC):
                packed[r, 4 * f : 4 * f + 4, :] = old[f, pl.ds(base, 4, stride=8), :]
        return 0

    lax.fori_loop(0, ROWS // 4, body, 0)


def split_marks(marks):
    return (
        jnp.broadcast_to(marks[:, 0:1], (128, 128)),
        jnp.broadcast_to(marks[:, 64:65], (128, 128)),
    )


def arrived_rows(marks, idx_v):
    even = lax.broadcasted_iota(jnp.int32, (128, 128), 0).astype(F32) * 2.0
    mark0, mark1 = split_marks(marks)
    nf = lane_iota(128).astype(F32)
    idx = jnp.where(mark0 == nf, even, 0.0) + jnp.where(mark1 == nf, even + 1.0, 0.0)
    idx = jnp.sum(idx, axis=0, keepdims=True)
    idx_v[...] = idx.astype(jnp.int32)


def unpack_chunk(idx_s, recv, placed, first):
    def body(col, _):
        for layer in range(16):
            a = idx_s[0, col * 16 + layer] & (ROWS - 1)
            start = (layer // 8) * 32 + layer % 8
            for f in range(FPC):
                placed[col, first + f, pl.ds(start, 4, stride=8), :] = recv[
                    a, 4 * f : 4 * f + 4, :
                ]
        return 0

    lax.fori_loop(0, 8, body, 0)


def whole_kernel(place_far, old, vx, vs, vw, valx, vals, valw, placed, out, tail, pos_v, scratch):
    (
        idx_v, idx_s, pos_s, marks, marks_in, olds, packs, recvs,
        pad, mat, mat_t, coef, wval, dcol, points, faces, faces_in, boxes, half,
        planes, planes_in, sums, wires, smalls, tsem, ssem, rsem, msem, hssem, hrsem, osem, lsem, isem,
    ) = scratch
    recvs = list(recvs) + [tail]
    place, *tables = smalls
    place_load = pltpu.make_async_copy(place_far, place, tsem.at[6])
    place_load.start()
    table_loads = [
        pltpu.make_async_copy(value, table, tsem.at[i])
        for i, (value, table) in enumerate(zip((vx, vs, vw, valx, vals, valw), tables))
    ]
    gx, gy = my_place()
    me = gx * 8 + gy
    everyone = peers(ORDER)
    last = peers(LAST)
    last = last[1:] + last[:1]
    barrier = pltpu.get_barrier_semaphore()
    loads = [
        pltpu.make_async_copy(old.at[pl.ds(FPC * ch, FPC)], olds[ch], osem.at[ch])
        for ch in range(NCH)
    ]

    for peer in last:
        pl.semaphore_signal(barrier, inc=1, device_id=peer, device_id_type=MESH)
    for copy in loads + table_loads:
        copy.start()
    place_load.wait()
    target_rows(place[...], idx_v, marks)
    copy = pltpu.make_async_copy(idx_v, idx_s, isem.at[0])
    copy.start()
    copy.wait()
    own = []

    def pack(ch):
        loads[ch].wait()
        pack_chunk(idx_s, olds[ch], packs[ch])

    def send_one(source, target, send_sem, recv_sem, peer):
        d = peer[0] * 8 + peer[1]
        pltpu.make_async_remote_copy(
            source.at[pl.ds(2 * d, 2)],
            target.at[pl.ds(2 * me, 2)],
            send_sem,
            recv_sem,
            device_id=peer,
            device_id_type=MESH,
        ).start()

    def send_marks(peer):
        pltpu.make_async_remote_copy(
            marks.at[pl.ds(peer[0] * 8 + peer[1], 1)],
            marks_in.at[pl.ds(me, 1)],
            msem.at[0],
            msem.at[1],
            device_id=peer,
            device_id_type=MESH,
        ).start()

    def keep_own(source, target, sem):
        copy = pltpu.make_async_copy(
            source.at[pl.ds(2 * me, 2)], target.at[pl.ds(2 * me, 2)], sem
        )
        copy.start()
        own.append(copy)

    def send(ch):
        for peer in everyone if ch < NCH - 1 else last:
            send_one(packs[ch], recvs[ch], ssem.at[ch], rsem.at[ch], peer)
        keep_own(packs[ch], recvs[ch], lsem.at[ch])

    some = pl.ds(0, ROWS - 2)

    def arrive(ch):
        pltpu.make_async_copy(packs[ch].at[some], recvs[ch].at[some], rsem.at[ch]).wait()
        own[ch].wait()

    def unpack(ch):
        unpack_chunk(pos_s, recvs[ch], placed, FPC * ch)

    pack(0)
    pl.semaphore_wait(barrier, 127)
    send(0)
    for peer in everyone:
        send_marks(peer)
    pack(1)
    send(1)
    own_marks = pltpu.make_async_copy(
        marks.at[pl.ds(me, 1)], marks_in.at[pl.ds(me, 1)], lsem.at[NCH]
    )
    own_marks.start()
    pack(2)
    send(2)
    for ch in range(3, NCH):
        pack(ch)
    for copy in table_loads:
        copy.wait()
    build_tables(*tables, pad, mat, mat_t, coef, wval, dcol)
    pltpu.make_async_copy(marks.at[pl.ds(0, 127)], marks_in.at[pl.ds(0, 127)], msem.at[1]).wait()
    own_marks.wait()
    marks_here = marks_in[...].reshape(128, 128)
    arrived_rows(marks_here, pos_v)
    copy = pltpu.make_async_copy(pos_v, pos_s, isem.at[1])
    copy.start()
    copy.wait()
    arrive(0)
    arrive(1)
    right_side([recvs[ch].reshape(ROWS * W, 128) for ch in range(2)], marks_here, points)
    gather_planes(points, faces)
    reads = (
        lambda at, n: points[448 + at : 448 + at + n, :],
        lambda at, n: points[at : at + n, :],
        lambda at, n: faces[0, at : at + n, :],
        lambda at, n: faces[1, at : at + n, :],
    )
    for p in range(4):
        squeeze_plane(p, reads[p], wires[p])
    halo = plane_copies(wires[0:4], wires[4:8], hssem, hrsem, 0)
    for copy in halo:
        copy.start()
    send(3)
    fill_inner(points, boxes)
    unpack(0)
    unpack(1)
    for p, copy in enumerate(halo):
        copy.wait()
        widen_plane(p, wires[4 + p], faces_in)
    fill_faces(points, faces, faces_in, boxes)
    solve_boxes(boxes, half, mat, mat_t, coef, wval, dcol)
    return_planes(boxes, planes)
    for p in range(4):
        squeeze_plane(p, lambda at, n, p=p: planes[p, at : at + n, :], wires[8 + p])
    halo = plane_copies(wires[8:12], wires[12:16], hssem, hrsem, 4)
    for copy in halo:
        copy.start()
    send(4)
    send(5)
    arrive(2)
    unpack(2)
    for p, copy in enumerate(halo):
        copy.wait()
        widen_plane(p, wires[12 + p], planes_in)
    sum_cells(planes, planes_in, boxes, sums, out)
    for ch in range(3, NCH - 1):
        arrive(ch)
        unpack(ch)
    arrive(NCH - 1)
    pltpu.make_async_copy(marks.at[pl.ds(0, 127)], marks_in.at[pl.ds(0, 127)], msem.at[0]).wait()
    for ch in range(NCH):
        pltpu.make_async_copy(packs[ch].at[some], recvs[ch].at[some], ssem.at[ch]).wait()


def publish_kernel(placed, correction, tail, pos_v, new_states, out, stage, pos_s, sems):
    index = pltpu.make_async_copy(pos_v, pos_s, sems.at[17])
    index.start()
    done = FIELDS - FPC
    copies = [
        pltpu.make_async_copy(placed.at[c], new_states.at[c, pl.ds(0, done)], sems.at[c])
        for c in range(8)
    ]
    copies.append(pltpu.make_async_copy(correction, out, sems.at[16]))
    for copy in copies:
        copy.start()
    index.wait()
    unpack_chunk(pos_s, tail, stage, 0)
    for c in range(8):
        copies.append(
            pltpu.make_async_copy(stage.at[c], new_states.at[c, pl.ds(done, FPC)], sems.at[8 + c])
        )
        copies[-1].start()
    for copy in copies:
        copy.wait()


SCRATCH = (
    pltpu.VMEM((1, ROWS), jnp.int32),
    pltpu.SMEM((1, ROWS), jnp.int32),
    pltpu.SMEM((1, 128), jnp.int32),
    pltpu.VMEM((128, 1, 128), F32),
    pltpu.VMEM((128, 1, 128), F32),
    [pltpu.VMEM((FPC, ROWS * 4, 128), F32)] * NCH,
    [pltpu.VMEM((ROWS, W, 128), F32)] * NCH,
    [pltpu.VMEM((ROWS, W, 128), F32)] * (NCH - 1),
    pltpu.VMEM((16, 128), F32),
    pltpu.VMEM((128, 128), F32),
    pltpu.VMEM((128, 128), F32),
    pltpu.VMEM((10, 10, 8, 128), F32),
    pltpu.VMEM((10, 8, 128), F32),
    pltpu.VMEM((128, 128), F32),
    pltpu.VMEM((512, 128), F32),
    pltpu.VMEM((2, 64, 128), F32),
    pltpu.VMEM((4, 64, 128), F32),
    pltpu.VMEM((128, 1280), F32),
    pltpu.VMEM((128, 1280), F32),
    pltpu.VMEM((4, 64, 128), F32),
    pltpu.VMEM((4, 64, 128), F32),
    pltpu.VMEM((8, 64, 128), F32),
    [pltpu.VMEM((rows, 128), F32) for rows in (16, 16, 32, 32) * 4],
    [pltpu.VMEM((1, ROWS), jnp.int32)]
    + [pltpu.VMEM(s, F32) for s in ((10, 10), (10, 10), (10, 16, 10), (1, 10), (1, 10), (16, 10))],
    pltpu.SemaphoreType.DMA((7,)),
    pltpu.SemaphoreType.DMA((NCH,)),
    pltpu.SemaphoreType.DMA((NCH,)),
    pltpu.SemaphoreType.DMA((2,)),
    pltpu.SemaphoreType.DMA((8,)),
    pltpu.SemaphoreType.DMA((8,)),
    pltpu.SemaphoreType.DMA((NCH,)),
    pltpu.SemaphoreType.DMA((NCH + 1,)),
    pltpu.SemaphoreType.DMA((2,)),
)


def shards(old_states, new_place, vectors_x, vectors_s, vectors_w, values_x, values_s, values_w):
    old_view = old_states.transpose(1, 0, 2).reshape(FIELDS, 32, 8, 4, 128)
    old_view = old_view.transpose(0, 1, 3, 2, 4).reshape(FIELDS, ROWS * 4, 128)
    vmem = pl.BlockSpec(memory_space=pltpu.VMEM)
    far = pl.BlockSpec(memory_space=pl.ANY)
    results = pl.pallas_call(
        whole_kernel,
        in_specs=[far] * 8,
        out_specs=[vmem] * 4,
        out_shape=[
            pltpu.VMEM((8, FIELDS - FPC, 64, 128), F32),
            pltpu.VMEM((512, 128), F32),
            pltpu.VMEM((ROWS, W, 128), F32),
            pltpu.VMEM((1, 128), jnp.int32),
        ],
        scratch_shapes=[SCRATCH],
        compiler_params=pltpu.CompilerParams(
            collective_id=1, has_side_effects=True, vmem_limit_bytes=VMEM_LIMIT
        ),
        name="migrate_and_sweep",
    )(
        new_place.reshape(1, ROWS),
        old_view,
        vectors_x,
        vectors_s,
        vectors_w.transpose(1, 0, 2),
        values_x.reshape(1, 10),
        values_s.reshape(1, 10),
        values_w,
    )
    placed, correction = pl.pallas_call(
        publish_kernel,
        in_specs=[vmem] * 4,
        out_specs=[far] * 2,
        out_shape=[
            jax.ShapeDtypeStruct((8, FIELDS, 64, 128), F32),
            jax.ShapeDtypeStruct((512, 128), F32),
        ],
        scratch_shapes=[
            pltpu.VMEM((8, FPC, 64, 128), F32),
            pltpu.SMEM((1, 128), jnp.int32),
            pltpu.SemaphoreType.DMA((18,)),
        ],
        compiler_params=pltpu.CompilerParams(vmem_limit_bytes=VMEM_LIMIT),
        name="publish",
    )(*(pltpu.with_memory_space_constraint(r, pltpu.VMEM) for r in results))
    placed = placed.reshape(4, 2, FIELDS, 2, 4, 8, 128).transpose(0, 1, 3, 5, 2, 4, 6)
    return placed.reshape(4, 2, 16, FIELDS, 512), correction.reshape(32, 16, 128)


def solution(mesh):
    placed = (P(("gx", "gy"), None, None), P(("gx", "gy")), P(), P(), P(), P(), P(), P())
    return jax.shard_map(
        shards,
        mesh=mesh,
        in_specs=placed,
        out_specs=(P("gx", "gy", None, None, None), P("gx", "gy", None)),
        check_vma=False,
    )
```

```python
import functools
import jax
import jax.numpy as jnp
from jax import lax
from jax.experimental import pallas as pl
from jax.experimental.pallas import tpu as pltpu
from jax.sharding import PartitionSpec as P

MESH = pl.DeviceIdType.MESH
HIGHEST = lax.Precision.HIGHEST
F32 = jnp.float32

FIELDS = 12
FPC = 2
NCH = FIELDS // FPC
W = 4 * FPC
VMEM_LIMIT = 61_000_000
ROWS = 256


def send_order():
    left = [
        (a, b, c) for a in range(4) for b in range(4) for c in range(4) if (a, b, c) != (0, 0, 0)
    ]
    load = [0] * 6
    order = []

    def with_step(step):
        out = list(load)
        for axis, value in enumerate(step):
            if value in (1, 2):
                out[2 * axis] += 1
            if value in (2, 3):
                out[2 * axis + 1] += 1
        return out

    def cost(step):
        after = with_step(step)
        total = sum(after)
        return (6 * max(after) - total, sum(v * v for v in after) * 6 - total * total, step)

    while left:
        best = min(left, key=cost)
        left.remove(best)
        load[:] = with_step(best)
        order.append(best)
    return order


ORDER = send_order()
LAST = sorted(ORDER, key=lambda step: -sum(min(v, 4 - v) for v in step))


def my_place():
    gx = lax.axis_index("gx")
    gy = lax.axis_index("gy")
    return gx, gy


def peers(steps):
    gx, gy = my_place()
    x, z = gx // 4, lax.rem(gx, 4)
    y, core = gy // 2, lax.rem(gy, 2)
    other = 1 - core
    out = [(gx, y * 2 + other)]
    pairs = [(to, step) for to in (0, 1) for step in steps]
    if steps is LAST:
        pairs = [(to, step) for step in steps for to in (0, 1)]
    hops = [lax.rem(4 + d - 2 * d * core, 4) for d in range(4)]
    hops[2] = 2
    xs = [lax.rem(x + hop, 4) * 4 for hop in hops]
    zs = [lax.rem(z + hop, 4) for hop in hops]
    gxs = [[px + pz for pz in zs] for px in xs]
    ys = [lax.rem(y + hop, 4) * 2 for hop in hops]
    gys = [(py + core, py + other) for py in ys]
    for to, step in pairs:
        out.append((gxs[step[0]][step[2]], gys[step[1]][to]))
    return out


def lane_iota(rows):
    return lax.broadcasted_iota(jnp.int32, (rows, 128), 1)


def tile_of(k):
    return slice(k * 128, (k + 1) * 128)


def build_tables(vx, vs, vw, valx, vals, valw, pad, mat, mat_t, coef, wval, dcol):
    q = lax.broadcasted_iota(jnp.int32, (16, 128), 1)
    u_row = lax.broadcasted_iota(jnp.int32, (16, 128), 0)
    along = (q & 7) + 1
    u_of = jnp.where(q < 64, (q >> 3) + 1, jnp.where(q < 72, 0, jnp.where(q < 80, 9, along)))
    v_of = jnp.where(q < 80, along, jnp.where(q < 88, 0, 9))
    pick_u = jnp.where((u_row == u_of) & (q < 96), 1.0, 0.0)
    pick_v = jnp.where((u_row == v_of) & (q < 96), 1.0, 0.0)
    big_r = lax.broadcasted_iota(jnp.int32, (128, 128), 0)
    big_c = lax.broadcasted_iota(jnp.int32, (128, 128), 1)
    i_of = (big_r * 205) >> 11
    j_of = big_r - i_of * 10
    pick_i = jnp.where((big_c == i_of) & (big_r < 100), 1.0, 0.0)
    pick_j = jnp.where((big_c == j_of) & (big_r < 100), 1.0, 0.0)
    first = (((0,), (0,)), ((), ()))

    def padded(value, width=10):
        pad[...] = jnp.zeros((16, 128), F32)
        pad[0 : value.shape[0], 0:width] = value
        return pad[...]

    def grow(vec, pick_q, pick_row):
        side = lax.dot_general(
            padded(vec), pick_q, first, precision=HIGHEST, preferred_element_type=F32
        )
        return jnp.dot(pick_row, side, precision=HIGHEST, preferred_element_type=F32)

    both = grow(vx[...], pick_u, pick_i) * grow(vs[...], pick_v, pick_j)
    mat[...] = both
    mat_t[...] = both.T
    rows = padded(valx[...])[0:1, :]
    d = jnp.sum(pick_i * rows, axis=1, keepdims=True)
    rows = padded(vals[...])[0:1, :]
    d = d + jnp.sum(pick_j * rows, axis=1, keepdims=True)
    dcol[...] = jnp.broadcast_to(d, (128, 128))
    spread = jnp.where(u_row == (q & 15), 1.0, 0.0)
    for w in range(10):
        table = lax.dot_general(
            padded(vw[w]), spread, first, precision=HIGHEST, preferred_element_type=F32
        )
        for k in range(10):
            coef[w, k] = jnp.broadcast_to(table[k : k + 1, :], (8, 128))
    table = lax.dot_general(
        padded(valw[...]), spread, first, precision=HIGHEST, preferred_element_type=F32
    )
    for k in range(10):
        wval[k] = jnp.broadcast_to(table[k : k + 1, :], (8, 128))


def right_side(arrived, marks, points):
    nf = lane_iota(128).astype(F32)
    chosen = [jnp.where(mark == nf, 1.0, 0.0) for mark in split_marks(marks)]
    for c in range(4):
        total = None
        for slot in range(2):
            f0, f1, f2 = (
                arrived[f // FPC][
                    pl.ds(slot * W + 4 * (f % FPC) + c, 128, stride=2 * W), :
                ]
                for f in range(3)
            )
            rows = 3.0 * f0 - 3.0 * f1 + f2
            part = jnp.dot(
                rows.T, chosen[slot], precision=HIGHEST, preferred_element_type=F32
            )
            total = part if total is None else total + part
        points[128 * c : 128 * (c + 1), :] = total


def gather_planes(points, planes):
    for i in range(8):
        planes[0, 8 * i : 8 * i + 8, :] = points[64 * i + 56 : 64 * i + 64, :]
        planes[1, 8 * i : 8 * i + 8, :] = points[64 * i : 64 * i + 8, :]


def neighbours():
    gx, gy = my_place()
    return (
        (lax.rem(gx + 1, 16), gy),
        (lax.rem(gx + 15, 16), gy),
        (gx, lax.rem(gy + 1, 8)),
        (gx, lax.rem(gy + 7, 8)),
    )


def squeeze_plane(p, read, wire):
    lane = lane_iota(16)
    if p < 2:
        first = 96 if p == 0 else 0
        total = None
        for q in range(4):
            turn = (32 * q - first) % 128
            rows = read(16 * q, 16)
            rows = pltpu.roll(rows, turn, 1) if turn else rows
            total = rows if q == 0 else jnp.where((lane >> 5) == q, rows, total)
        wire[...] = total
    else:
        upper = (lane & 16) != 0
        for half in range(2):
            near, moved = read(16 * half, 16), read(32 + 16 * half, 16)
            moved = pltpu.roll(moved, 112 if p == 2 else 16, 1)
            keep = upper if p == 2 else ~upper
            wire[16 * half : 16 * half + 16, :] = jnp.where(keep, near, moved)


def widen_plane(p, wire, plane):
    if p < 2:
        first = 96 if p == 0 else 0
        for q in range(4):
            turn = (first - 32 * q) % 128
            rows = pltpu.roll(wire[...], turn, 1) if turn else wire[...]
            plane[p, 16 * q : 16 * q + 16, :] = rows
    else:
        plane[p, 0:32, :] = wire[...]
        plane[p, 32:64, :] = pltpu.roll(wire[...], 16 if p == 2 else 112, 1)


def plane_copies(sources, targets, ssem, rsem, base):
    return [
        pltpu.make_async_remote_copy(
            sources[p],
            targets[p],
            ssem.at[base + p],
            rsem.at[base + p],
            device_id=peer,
            device_id_type=MESH,
        )
        for p, peer in enumerate(neighbours())
    ]


def fill_inner(points, boxes):
    boxes[96:128, :] = jnp.zeros((32, 1280), F32)
    boxes[64:96, tile_of(0)] = jnp.zeros((32, 128), F32)
    boxes[64:96, tile_of(9)] = jnp.zeros((32, 128), F32)
    layer = lane_iota(64) & 15
    for k in range(8):
        value = points[pl.ds(k, 64, stride=8), :]
        boxes[0:64, tile_of(k + 1)] = value
        if k == 7:
            boxes[0:64, tile_of(0)] = jnp.where(layer == 0, 0.0, pltpu.roll(value, 1, 1))
        if k == 0:
            boxes[0:64, tile_of(9)] = jnp.where(layer == 15, 0.0, pltpu.roll(value, 127, 1))


def fill_faces(points, planes, arrived, boxes):
    lane = lane_iota(8)
    upper = (lane & 16) != 0
    for k in range(8):
        own = points[pl.ds(448 + k, 8, stride=8), :]
        far = arrived[0, pl.ds(k, 8, stride=8), :]
        boxes[64:72, tile_of(k + 1)] = pltpu.roll(jnp.where(lane >= 96, far, own), 32, 1)
        own = points[pl.ds(k, 8, stride=8), :]
        far = arrived[1, pl.ds(k, 8, stride=8), :]
        boxes[72:80, tile_of(k + 1)] = pltpu.roll(jnp.where(lane < 32, far, own), 96, 1)
        own = planes[0, pl.ds(k, 8, stride=8), :]
        far = arrived[2, pl.ds(k, 8, stride=8), :]
        boxes[80:88, tile_of(k + 1)] = jnp.where(
            upper, pltpu.roll(own, 16, 1), pltpu.roll(far, 112, 1)
        )
        own = planes[1, pl.ds(k, 8, stride=8), :]
        far = arrived[3, pl.ds(k, 8, stride=8), :]
        boxes[88:96, tile_of(k + 1)] = jnp.where(
            upper, pltpu.roll(far, 16, 1), pltpu.roll(own, 112, 1)
        )


def solve_boxes(boxes, half, mat, mat_t, coef, wval, dcol):
    half[0:104, :] = jnp.dot(
        mat[0:104, :], boxes[...], precision=HIGHEST, preferred_element_type=F32
    )
    half[104:128, :] = jnp.zeros((24, 1280), F32)

    def rows(t, _):
        at = pl.ds(pl.multiple_of(t * 8, 8), 8)
        section = [half[at, tile_of(w)] for w in range(10)]
        modal = []
        for k in range(10):
            total = coef[0, k] * section[0]
            for w in range(1, 10):
                total = total + coef[w, k] * section[w]
            modal.append(total / (dcol[at, :] + wval[k]))
        for w in range(10):
            total = coef[w, 0] * modal[0]
            for k in range(1, 10):
                total = total + coef[w, k] * modal[k]
            half[at, tile_of(w)] = total
        return 0

    lax.fori_loop(0, 13, rows, 0)
    boxes[0:96, :] = jnp.dot(
        mat_t[0:96, :], half[...], precision=HIGHEST, preferred_element_type=F32
    )


def return_planes(boxes, planes):
    for p, first in enumerate((72, 64, 88, 80)):
        for k in range(8):
            planes[p, pl.ds(k, 8, stride=8), :] = boxes[first : first + 8, tile_of(k + 1)]


def sum_cells(planes, arrived, boxes, sums, out):
    lane = lane_iota(8)
    upper = (lane & 16) != 0
    layer = lane_iota(64) & 15
    for k in range(8):
        value = boxes[0:64, tile_of(k + 1)]
        if k == 7:
            value = value + jnp.where(
                layer == 15, 0.0, pltpu.roll(boxes[0:64, tile_of(0)], 127, 1)
            )
        if k == 0:
            value = value + jnp.where(layer == 0, 0.0, pltpu.roll(boxes[0:64, tile_of(9)], 1, 1))
        sums[k] = value
        at = pl.ds(k, 8, stride=8)
        own, far = planes[0, at, :], arrived[0, at, :]
        sums[k, 0:8, :] += pltpu.roll(jnp.where(lane >= 96, far, own), 32, 1)
        own, far = planes[1, at, :], arrived[1, at, :]
        sums[k, 56:64, :] += pltpu.roll(jnp.where(lane < 32, far, own), 96, 1)
        own, far = planes[2, at, :], arrived[2, at, :]
        sums[k, pl.ds(0, 8, stride=8), :] += jnp.where(
            upper, pltpu.roll(own, 16, 1), pltpu.roll(far, 112, 1)
        )
        own, far = planes[3, at, :], arrived[3, at, :]
        sums[k, pl.ds(7, 8, stride=8), :] += jnp.where(
            upper, pltpu.roll(far, 16, 1), pltpu.roll(own, 112, 1)
        )
    src = lax.broadcasted_iota(jnp.int32, (128, 128), 0)
    to = lax.broadcasted_iota(jnp.int32, (128, 128), 1)
    order = jnp.where(to == (src & 15) * 8 + (src >> 4), 1.0, 0.0)
    group = lane_iota(64) >> 4
    for b in range(8):
        mixed = jnp.zeros((64, 128), F32)
        for k in range(8):
            turned = pltpu.roll(sums[k], ((k - b) % 8) * 16, 1) if k != b else sums[k]
            mixed = jnp.where(group == k, turned, mixed)
        mixed = jnp.dot(mixed, order, precision=HIGHEST, preferred_element_type=F32)
        for i in range(8):
            first = ((b // 2) * 8 + i) * 16 + (b % 2) * 8
            out[first : first + 8, :] = mixed[8 * i : 8 * i + 8, :]


def target_rows(place, idx_v, marks):
    live = place >= 0
    p = jnp.maximum(place, 0)
    layer = p & 15
    es = (p >> 4) & 15
    ex = p >> 8
    target = ((ex >> 2) * 8 + (es >> 1)).astype(F32)
    row = (((ex & 3) * 2 + (es & 1)) * 16 + layer).astype(F32)
    key = jnp.where(live, target, -1.0)
    ri = lax.broadcasted_iota(jnp.int32, (ROWS, ROWS), 0)
    ci = lax.broadcasted_iota(jnp.int32, (ROWS, ROWS), 1)
    rf = ri.astype(F32)
    cf = ci.astype(F32)
    same = ri == ci
    key_b = jnp.broadcast_to(key, (ROWS, ROWS))
    key_c = jnp.sum(jnp.where(same, key_b, 0.0), axis=1, keepdims=True)
    rank = jnp.sum(jnp.where((key_c == key_b) & (ri < ci), 1.0, 0.0), axis=0, keepdims=True)
    pos = jnp.where(live, target * 2.0 + rank, -1.0)
    pos_b = jnp.broadcast_to(pos, (ROWS, ROWS))
    pos_c = jnp.sum(jnp.where(same, pos_b, 0.0), axis=1, keepdims=True)
    idx = jnp.sum(jnp.where(pos_c == cf, rf, 0.0), axis=0, keepdims=True)
    idx_v[...] = idx.astype(jnp.int32)
    row_b = jnp.broadcast_to(row + 1.0, (128, ROWS))
    pos_b = jnp.broadcast_to(pos, (128, ROWS))
    even = lax.broadcasted_iota(jnp.int32, (128, ROWS), 0).astype(F32) * 2.0
    mark0 = jnp.sum(jnp.where(pos_b == even, row_b, 0.0), axis=1, keepdims=True) - 1.0
    mark1 = jnp.sum(jnp.where(pos_b == even + 1.0, row_b, 0.0), axis=1, keepdims=True) - 1.0
    both = jnp.where(lane_iota(128) < 64, mark0, mark1)
    marks[...] = both.reshape(128, 1, 128)


def pack_chunk(idx_s, old, packed):
    def body(step, _):
        for more in range(4):
            r = step * 4 + more
            s = idx_s[0, r] & (ROWS - 1)
            base = (s >> 3) * 32 + (s & 7)
            for f in range(FPC):
                packed[r, 4 * f : 4 * f + 4, :] = old[f, pl.ds(base, 4, stride=8), :]
        return 0

    lax.fori_loop(0, ROWS // 4, body, 0)


def split_marks(marks):
    return (
        jnp.broadcast_to(marks[:, 0:1], (128, 128)),
        jnp.broadcast_to(marks[:, 64:65], (128, 128)),
    )


def arrived_rows(marks, idx_v):
    even = lax.broadcasted_iota(jnp.int32, (128, 128), 0).astype(F32) * 2.0
    mark0, mark1 = split_marks(marks)
    nf = lane_iota(128).astype(F32)
    idx = jnp.where(mark0 == nf, even, 0.0) + jnp.where(mark1 == nf, even + 1.0, 0.0)
    idx = jnp.sum(idx, axis=0, keepdims=True)
    idx_v[...] = idx.astype(jnp.int32)


def unpack_chunk(idx_s, recv, placed, first):
    def body(col, _):
        for layer in range(16):
            a = idx_s[0, col * 16 + layer] & (ROWS - 1)
            start = (layer // 8) * 32 + layer % 8
            for f in range(FPC):
                placed[col, first + f, pl.ds(start, 4, stride=8), :] = recv[
                    a, 4 * f : 4 * f + 4, :
                ]
        return 0

    lax.fori_loop(0, 8, body, 0)


def whole_kernel(place_far, old, vx, vs, vw, valx, vals, valw, placed, out, tail, pos_v, scratch):
    (
        idx_v, idx_s, pos_s, marks, marks_in, olds, packs, recvs,
        pad, mat, mat_t, coef, wval, dcol, points, faces, faces_in, boxes, half,
        planes, planes_in, sums, wires, smalls, tsem, ssem, rsem, msem, hssem, hrsem, osem, lsem, isem,
    ) = scratch
    recvs = list(recvs) + [tail]
    place, *tables = smalls
    place_load = pltpu.make_async_copy(place_far, place, tsem.at[6])
    place_load.start()
    table_loads = [
        pltpu.make_async_copy(value, table, tsem.at[i])
        for i, (value, table) in enumerate(zip((vx, vs, vw, valx, vals, valw), tables))
    ]
    gx, gy = my_place()
    me = gx * 8 + gy
    everyone = peers(ORDER)
    last = peers(LAST)
    last = last[1:] + last[:1]
    barrier = pltpu.get_barrier_semaphore()
    loads = [
        pltpu.make_async_copy(old.at[pl.ds(FPC * ch, FPC)], olds[ch], osem.at[ch])
        for ch in range(NCH)
    ]

    for peer in last:
        pl.semaphore_signal(barrier, inc=1, device_id=peer, device_id_type=MESH)
    for copy in loads + table_loads:
        copy.start()
    place_load.wait()
    target_rows(place[...], idx_v, marks)
    copy = pltpu.make_async_copy(idx_v, idx_s, isem.at[0])
    copy.start()
    copy.wait()
    own = []

    def pack(ch):
        loads[ch].wait()
        pack_chunk(idx_s, olds[ch], packs[ch])

    def send_one(source, target, send_sem, recv_sem, peer):
        d = peer[0] * 8 + peer[1]
        pltpu.make_async_remote_copy(
            source.at[pl.ds(2 * d, 2)],
            target.at[pl.ds(2 * me, 2)],
            send_sem,
            recv_sem,
            device_id=peer,
            device_id_type=MESH,
        ).start()

    def send_marks(peer):
        pltpu.make_async_remote_copy(
            marks.at[pl.ds(peer[0] * 8 + peer[1], 1)],
            marks_in.at[pl.ds(me, 1)],
            msem.at[0],
            msem.at[1],
            device_id=peer,
            device_id_type=MESH,
        ).start()

    def keep_own(source, target, sem):
        copy = pltpu.make_async_copy(
            source.at[pl.ds(2 * me, 2)], target.at[pl.ds(2 * me, 2)], sem
        )
        copy.start()
        own.append(copy)

    def send(ch):
        for peer in everyone if ch < NCH - 1 else last:
            send_one(packs[ch], recvs[ch], ssem.at[ch], rsem.at[ch], peer)
        keep_own(packs[ch], recvs[ch], lsem.at[ch])

    some = pl.ds(0, ROWS - 2)

    def arrive(ch):
        pltpu.make_async_copy(packs[ch].at[some], recvs[ch].at[some], rsem.at[ch]).wait()
        own[ch].wait()

    def unpack(ch):
        unpack_chunk(pos_s, recvs[ch], placed, FPC * ch)

    pack(0)
    pl.semaphore_wait(barrier, 127)
    send(0)
    for peer in everyone:
        send_marks(peer)
    pack(1)
    send(1)
    own_marks = pltpu.make_async_copy(
        marks.at[pl.ds(me, 1)], marks_in.at[pl.ds(me, 1)], lsem.at[NCH]
    )
    own_marks.start()
    pack(2)
    send(2)
    for ch in range(3, NCH):
        pack(ch)
    for copy in table_loads:
        copy.wait()
    build_tables(*tables, pad, mat, mat_t, coef, wval, dcol)
    pltpu.make_async_copy(marks.at[pl.ds(0, 127)], marks_in.at[pl.ds(0, 127)], msem.at[1]).wait()
    own_marks.wait()
    marks_here = marks_in[...].reshape(128, 128)
    arrived_rows(marks_here, pos_v)
    copy = pltpu.make_async_copy(pos_v, pos_s, isem.at[1])
    copy.start()
    copy.wait()
    arrive(0)
    arrive(1)
    right_side([recvs[ch].reshape(ROWS * W, 128) for ch in range(2)], marks_here, points)
    gather_planes(points, faces)
    reads = (
        lambda at, n: points[448 + at : 448 + at + n, :],
        lambda at, n: points[at : at + n, :],
        lambda at, n: faces[0, at : at + n, :],
        lambda at, n: faces[1, at : at + n, :],
    )
    for p in range(4):
        squeeze_plane(p, reads[p], wires[p])
    halo = plane_copies(wires[0:4], wires[4:8], hssem, hrsem, 0)
    for copy in halo:
        copy.start()
    send(3)
    fill_inner(points, boxes)
    unpack(0)
    unpack(1)
    for p, copy in enumerate(halo):
        copy.wait()
        widen_plane(p, wires[4 + p], faces_in)
    fill_faces(points, faces, faces_in, boxes)
    solve_boxes(boxes, half, mat, mat_t, coef, wval, dcol)
    return_planes(boxes, planes)
    for p in range(4):
        squeeze_plane(p, lambda at, n, p=p: planes[p, at : at + n, :], wires[8 + p])
    halo = plane_copies(wires[8:12], wires[12:16], hssem, hrsem, 4)
    for copy in halo:
        copy.start()
    send(4)
    send(5)
    arrive(2)
    unpack(2)
    for p, copy in enumerate(halo):
        copy.wait()
        widen_plane(p, wires[12 + p], planes_in)
    sum_cells(planes, planes_in, boxes, sums, out)
    for ch in range(3, NCH - 1):
        arrive(ch)
        unpack(ch)
    arrive(NCH - 1)
    pltpu.make_async_copy(marks.at[pl.ds(0, 127)], marks_in.at[pl.ds(0, 127)], msem.at[0]).wait()
    for ch in range(NCH):
        pltpu.make_async_copy(packs[ch].at[some], recvs[ch].at[some], ssem.at[ch]).wait()


def publish_kernel(placed, correction, tail, pos_v, new_states, out, stage, pos_s, sems):
    index = pltpu.make_async_copy(pos_v, pos_s, sems.at[17])
    index.start()
    done = FIELDS - FPC
    copies = [
        pltpu.make_async_copy(placed.at[c], new_states.at[c, pl.ds(0, done)], sems.at[c])
        for c in range(8)
    ]
    copies.append(pltpu.make_async_copy(correction, out, sems.at[16]))
    for copy in copies:
        copy.start()
    index.wait()
    unpack_chunk(pos_s, tail, stage, 0)
    for c in range(8):
        copies.append(
            pltpu.make_async_copy(stage.at[c], new_states.at[c, pl.ds(done, FPC)], sems.at[8 + c])
        )
        copies[-1].start()
    for copy in copies:
        copy.wait()


SCRATCH = (
    pltpu.VMEM((1, ROWS), jnp.int32),
    pltpu.SMEM((1, ROWS), jnp.int32),
    pltpu.SMEM((1, 128), jnp.int32),
    pltpu.VMEM((128, 1, 128), F32),
    pltpu.VMEM((128, 1, 128), F32),
    [pltpu.VMEM((FPC, ROWS * 4, 128), F32)] * NCH,
    [pltpu.VMEM((ROWS, W, 128), F32)] * NCH,
    [pltpu.VMEM((ROWS, W, 128), F32)] * (NCH - 1),
    pltpu.VMEM((16, 128), F32),
    pltpu.VMEM((128, 128), F32),
    pltpu.VMEM((128, 128), F32),
    pltpu.VMEM((10, 10, 8, 128), F32),
    pltpu.VMEM((10, 8, 128), F32),
    pltpu.VMEM((128, 128), F32),
    pltpu.VMEM((512, 128), F32),
    pltpu.VMEM((2, 64, 128), F32),
    pltpu.VMEM((4, 64, 128), F32),
    pltpu.VMEM((128, 1280), F32),
    pltpu.VMEM((128, 1280), F32),
    pltpu.VMEM((4, 64, 128), F32),
    pltpu.VMEM((4, 64, 128), F32),
    pltpu.VMEM((8, 64, 128), F32),
    [pltpu.VMEM((rows, 128), F32) for rows in (16, 16, 32, 32) * 4],
    [pltpu.VMEM((1, ROWS), jnp.int32)]
    + [pltpu.VMEM(s, F32) for s in ((10, 10), (10, 10), (10, 16, 10), (1, 10), (1, 10), (16, 10))],
    pltpu.SemaphoreType.DMA((7,)),
    pltpu.SemaphoreType.DMA((NCH,)),
    pltpu.SemaphoreType.DMA((NCH,)),
    pltpu.SemaphoreType.DMA((2,)),
    pltpu.SemaphoreType.DMA((8,)),
    pltpu.SemaphoreType.DMA((8,)),
    pltpu.SemaphoreType.DMA((NCH,)),
    pltpu.SemaphoreType.DMA((NCH + 1,)),
    pltpu.SemaphoreType.DMA((2,)),
)


def shards(old_states, new_place, vectors_x, vectors_s, vectors_w, values_x, values_s, values_w):
    old_view = old_states.transpose(1, 0, 2).reshape(FIELDS, 32, 8, 4, 128)
    old_view = old_view.transpose(0, 1, 3, 2, 4).reshape(FIELDS, ROWS * 4, 128)
    vmem = pl.BlockSpec(memory_space=pltpu.VMEM)
    far = pl.BlockSpec(memory_space=pl.ANY)
    results = pl.pallas_call(
        whole_kernel,
        in_specs=[far] * 8,
        out_specs=[vmem] * 4,
        out_shape=[
            pltpu.VMEM((8, FIELDS - FPC, 64, 128), F32),
            pltpu.VMEM((512, 128), F32),
            pltpu.VMEM((ROWS, W, 128), F32),
            pltpu.VMEM((1, 128), jnp.int32),
        ],
        scratch_shapes=[SCRATCH],
        compiler_params=pltpu.CompilerParams(
            collective_id=1, has_side_effects=True, vmem_limit_bytes=VMEM_LIMIT
        ),
        name="migrate_and_sweep",
    )(
        new_place.reshape(1, ROWS),
        old_view,
        vectors_x,
        vectors_s,
        vectors_w.transpose(1, 0, 2),
        values_x.reshape(1, 10),
        values_s.reshape(1, 10),
        values_w,
    )
    placed, correction = pl.pallas_call(
        publish_kernel,
        in_specs=[vmem] * 4,
        out_specs=[far] * 2,
        out_shape=[
            jax.ShapeDtypeStruct((8, FIELDS, 64, 128), F32),
            jax.ShapeDtypeStruct((512, 128), F32),
        ],
        scratch_shapes=[
            pltpu.VMEM((8, FPC, 64, 128), F32),
            pltpu.SMEM((1, 128), jnp.int32),
            pltpu.SemaphoreType.DMA((18,)),
        ],
        compiler_params=pltpu.CompilerParams(vmem_limit_bytes=VMEM_LIMIT),
        name="publish",
    )(*(pltpu.with_memory_space_constraint(r, pltpu.VMEM) for r in results))
    placed = placed.reshape(4, 2, FIELDS, 2, 4, 8, 128).transpose(0, 1, 3, 5, 2, 4, 6)
    return placed.reshape(4, 2, 16, FIELDS, 512), correction.reshape(32, 16, 128)


def solution(mesh):
    placed = (P(("gx", "gy"), None, None), P(("gx", "gy")), P(), P(), P(), P(), P(), P())
    return jax.shard_map(
        shards,
        mesh=mesh,
        in_specs=placed,
        out_specs=(P("gx", "gy", None, None, None), P("gx", "gy", None)),
        check_vma=False,
    )
```
